256 devices in a mesh: member: 4 (over x_lo, core), row: 8 (over y, x_hi), rep: 8 (over z).
Axes of the slice: x: 4 (x_hi: 2, x_lo: 2; x = x_hi * 2 + x_lo), y: 4, z: 8, core: 2. Of those that a mesh axis runs over, the one named last changes fastest.
Arguments:
- features: bfloat16 [4, 32768, 256], P('member', ('row', 'rep')), may hold values from -6 to 6
- weights: bfloat16 [4, 256, 256], P('member'), may hold values from -0.375 to 0.375
- tile_values: bfloat16 [8, 8, 256, 128, 128], P('row', 'rep'), may hold values from -0.125 to 0.125
- tile_rows: int32 [8, 8, 256], P('row', 'rep'), may hold values from 0 to 31
- tile_cols: int32 [8, 8, 256], P('row', 'rep'), may hold values from 0 to 31
- tile_counts: int32 [8, 8], P('row', 'rep'), may hold values from 1 to 256, as said below
- labels: int32 [32768], P('row'), may hold values from 0 to 255
Outputs:
- mean_logits: float32 [32768, 256], P(('row', 'rep'))
- weight_grad: float32 [4, 256, 256], P('member')
- input_grad: bfloat16 [4, 32768, 256], P('member', ('row', 'rep'))
The draws below stay inside these ranges and needn't reach their ends.
Inputs may be any that keep to these rules, and one draw needn't show every extreme that they name: `tile_counts`: 256 on at least one index of row and rep in every draw; slots at or past a count are unused. `tile_rows`: places may repeat. `tile_cols`: places may repeat.
All inputs are finite; a program needn't handle non-finite values.
Results may differ from the reference program's by a relative error of at most 0.0058.
Values may be sent and summed in bfloat16 or wider, within the bound.
No kernel may reach another device: no remote copies, remote signals or barrier semaphores. Data moves between devices by JAX's collectives and lax.ppermute only.
A program may use at most 128 MiB of HBM per device.

```python
import math
import jax
import jax.numpy as jnp
from jax import lax

F = 256
K = 256
TILE = 128
NODE_DEV = 512
TILES_DEV = 256
MEMBERS = 4
NODES = 32768
N_ROW = 8
N_REP = 8


def draw_tile_counts(key, part):
    first_draw = jax.random.randint(jax.random.fold_in(key, 11), (N_ROW * N_REP,), 1, TILES_DEV + 1)
    second_draw = jax.random.randint(jax.random.fold_in(key, 12), (N_ROW * N_REP,), 1, TILES_DEV + 1)
    counts_flat = jnp.minimum(first_draw * second_draw // TILES_DEV + 1, TILES_DEV)
    chosen = jax.random.randint(jax.random.fold_in(key, 13), (), 0, N_ROW * N_REP)
    counts_flat = jnp.where(jnp.arange(N_ROW * N_REP, dtype=jnp.int32) == chosen, TILES_DEV, counts_flat)
    return counts_flat.reshape(N_ROW, N_REP).astype(jnp.int32)


def touch_ends(result, own_key, smallest, top_value):
    longest = result.shape.index(max(result.shape))
    spots = []
    for shift in (0, 1):
        where = [jax.random.randint(jax.random.fold_in(own_key, axis), (), 0, length) for axis, length in enumerate(result.shape)]
        where[longest] = (where[longest] + shift) % result.shape[longest]
        spots.append(tuple(where))
    return result.at[spots[0]].set(smallest).at[spots[1]].set(top_value)


def steps_of(stream_key, extent, split, smallest, top_value):
    def one(dim, parts):
        heights = jax.random.uniform(jax.random.fold_in(jax.random.fold_in(stream_key, 6), dim), (parts,), jnp.float32, smallest / len(split), top_value / len(split))
        return jnp.repeat(jnp.exp(heights), extent[dim] // parts).reshape((-1,) + (1,) * (len(extent) - dim - 1))

    gain = one(*split[0])
    for cut in split[1:]:
        gain = gain * one(*cut)
    return gain


def scatter_about(rng, extent, width, most, shards=(), kind=jnp.bfloat16):
    drawn = width * jax.random.normal(rng, extent, jnp.float32)
    if shards:
        drawn = drawn * steps_of(rng, extent, shards, -0.22, 0.18)
    return jnp.clip(drawn, -most, most).astype(kind)


def setup_inputs(seed: int = 0) -> dict:
    keys = jax.random.split(jax.random.key(seed), 8)
    features = scatter_about(keys[0], (MEMBERS, NODES, F), 1.0, 6.0, ((0, 4), (1, 64)))
    weights = scatter_about(keys[1], (MEMBERS, F, K), F ** -0.5, 0.375, ((0, 4),))
    tile_values = scatter_about(keys[2], (N_ROW, N_REP, TILES_DEV, TILE, TILE), (TILES_DEV * TILE * TILE // (4 * NODE_DEV)) ** -0.5, 0.125, ((0, 8), (1, 8)))
    tile_rows = touch_ends(jax.random.randint(keys[3], (N_ROW, N_REP, TILES_DEV), 0, NODE_DEV * N_REP // TILE), jax.random.fold_in(keys[3], 1), 0, (NODE_DEV * N_REP // TILE) - 1).astype(jnp.int32)
    tile_cols = touch_ends(jax.random.randint(keys[4], (N_ROW, N_REP, TILES_DEV), 0, NODE_DEV * N_ROW // TILE), jax.random.fold_in(keys[4], 1), 0, (NODE_DEV * N_ROW // TILE) - 1).astype(jnp.int32)
    tile_counts = draw_tile_counts(jax.random.fold_in(keys[7], 71), 0)
    labels = touch_ends(jax.random.randint(keys[6], (NODES,), 0, K), jax.random.fold_in(keys[6], 1), 0, K - 1).astype(jnp.int32)
    return dict(features=features, weights=weights, tile_values=tile_values, tile_rows=tile_rows, tile_cols=tile_cols, tile_counts=tile_counts, labels=labels)


group_tiles = 32

def reference(features, weights, tile_values, tile_rows, tile_cols, tile_counts, labels):
    group_rows = NODE_DEV * N_REP
    row_tiles = group_rows // TILE
    col_tiles = NODE_DEV * N_ROW // TILE
    blocks = TILES_DEV // group_tiles
    devices = N_ROW * N_REP
    feats_wide = features.astype(jnp.float32).reshape(MEMBERS, N_ROW, N_REP, NODE_DEV, F)
    flat_values = tile_values.reshape(devices, TILES_DEV, TILE, TILE)
    flat_rows = tile_rows.reshape(devices, TILES_DEV)
    flat_cols = tile_cols.reshape(devices, TILES_DEV)
    flat_counts = tile_counts.reshape(devices)
    slot_iota = jnp.arange(group_tiles, dtype=jnp.int32)
    row_iota = jnp.arange(row_tiles, dtype=jnp.int32)
    col_iota = jnp.arange(col_tiles, dtype=jnp.int32)
    high = lax.Precision.HIGHEST

    def forward_device(totals, device):
        row_index = device // N_REP
        rep_index = device % N_REP
        panel = jnp.take(feats_wide, rep_index, axis=2).reshape(MEMBERS, col_tiles, TILE, F)
        dev_values = jnp.take(flat_values, device, axis=0)
        dev_rows = jnp.take(flat_rows, device, axis=0)
        dev_cols = jnp.take(flat_cols, device, axis=0)
        dev_count = jnp.take(flat_counts, device, axis=0)

        def block_step(part, block_index):
            first_slot = block_index * group_tiles
            block_values = lax.dynamic_slice_in_dim(dev_values, first_slot, group_tiles, 0).astype(jnp.float32)
            rows_block = lax.dynamic_slice_in_dim(dev_rows, first_slot, group_tiles, 0)
            cols_block = lax.dynamic_slice_in_dim(dev_cols, first_slot, group_tiles, 0)
            live_mask = (first_slot + slot_iota < dev_count).astype(jnp.float32)
            picked = jnp.take(panel, cols_block, axis=1)
            product = jnp.einsum('bij,mbjf->mbif', block_values, picked, precision=high)
            product = product * live_mask[None, :, None, None]
            placing = (rows_block[:, None] == row_iota[None, :]).astype(jnp.float32)
            return (part + jnp.einsum('br,mbif->mrif', placing, product, precision=high), None)
        start_part = jnp.zeros((MEMBERS, row_tiles, TILE, F), jnp.float32)
        part, _ = lax.scan(block_step, start_part, jnp.arange(blocks, dtype=jnp.int32))
        part = part.reshape(MEMBERS, 1, group_rows, F)
        current = lax.dynamic_slice_in_dim(totals, row_index, 1, 1)
        totals = lax.dynamic_update_slice_in_dim(totals, current + part, row_index, 1)
        return (totals, None)
    start_totals = jnp.zeros((MEMBERS, N_ROW, group_rows, F), jnp.float32)
    aggregated, _ = lax.scan(forward_device, start_totals, jnp.arange(devices, dtype=jnp.int32))
    aggregated = aggregated.reshape(MEMBERS, NODES, F)
    weights_wide = weights.astype(jnp.float32)
    mean_logits = jnp.einsum('mnf,mfk->nk', aggregated, weights_wide, precision=high) / MEMBERS
    targets = (labels[:, None] == jnp.arange(K, dtype=jnp.int32)[None, :]).astype(jnp.float32)
    grad_logits = (jax.nn.sigmoid(mean_logits) - targets).astype(jnp.bfloat16)
    grad_wide = grad_logits.astype(jnp.float32)
    weight_grad = jnp.einsum('mnf,nk->mfk', aggregated, grad_wide, precision=high) / math.sqrt(NODES)
    spread = jnp.einsum('nk,mfk->mnf', grad_wide, weights_wide, precision=high).astype(jnp.bfloat16)
    spread = lax.optimization_barrier(spread).astype(jnp.float32)
    spread_groups = spread.reshape(MEMBERS, N_ROW, row_tiles, TILE, F)

    def backward_device(totals, device):
        row_index = device // N_REP
        rep_index = device % N_REP
        source_tiles = jnp.take(spread_groups, row_index, axis=1)
        dev_values = jnp.take(flat_values, device, axis=0)
        dev_rows = jnp.take(flat_rows, device, axis=0)
        dev_cols = jnp.take(flat_cols, device, axis=0)
        dev_count = jnp.take(flat_counts, device, axis=0)

        def block_step(part, block_index):
            first_slot = block_index * group_tiles
            block_values = lax.dynamic_slice_in_dim(dev_values, first_slot, group_tiles, 0).astype(jnp.float32)
            rows_block = lax.dynamic_slice_in_dim(dev_rows, first_slot, group_tiles, 0)
            cols_block = lax.dynamic_slice_in_dim(dev_cols, first_slot, group_tiles, 0)
            live_mask = (first_slot + slot_iota < dev_count).astype(jnp.float32)
            picked = jnp.take(source_tiles, rows_block, axis=1)
            product = jnp.einsum('bji,mbjf->mbif', block_values, picked, precision=high)
            product = product * live_mask[None, :, None, None]
            placing = (cols_block[:, None] == col_iota[None, :]).astype(jnp.float32)
            return (part + jnp.einsum('bc,mbif->mcif', placing, product, precision=high), None)
        start_part = jnp.zeros((MEMBERS, col_tiles, TILE, F), jnp.float32)
        part, _ = lax.scan(block_step, start_part, jnp.arange(blocks, dtype=jnp.int32))
        part = part.reshape(MEMBERS, N_ROW, 1, NODE_DEV, F)
        current = lax.dynamic_slice_in_dim(totals, rep_index, 1, 2)
        totals = lax.dynamic_update_slice_in_dim(totals, current + part, rep_index, 2)
        return (totals, None)
    start_back = jnp.zeros((MEMBERS, N_ROW, N_REP, NODE_DEV, F), jnp.float32)
    back_sums, _ = lax.scan(backward_device, start_back, jnp.arange(devices, dtype=jnp.int32))
    input_grad = back_sums.reshape(MEMBERS, NODES, F).astype(jnp.bfloat16)
    return (mean_logits, weight_grad, input_grad)
```

```python
import functools
import math

import jax
import jax.numpy as jnp
from jax import lax
from jax.experimental import pallas as pl
from jax.experimental.pallas import tpu as pltpu
from jax.sharding import PartitionSpec as P


bf16 = jnp.bfloat16
f32 = jnp.float32
vmem = pl.BlockSpec(memory_space=pltpu.VMEM)
smem = pl.BlockSpec(memory_space=pltpu.SMEM)

block_tiles = 32
unroll = 8


def shift(value, axis, step):
    size = lax.axis_size(axis)
    return lax.ppermute(value, axis, [(j, (j + step) % size) for j in range(size)])


def gather_relative(value, axis):
    size = lax.axis_size(axis)
    return [value] + [shift(value, axis, k) for k in range(1, size)]


def exchange_relative(blocks, axis):
    return [blocks[0]] + [shift(blocks[k], axis, k) for k in range(1, len(blocks))]


def project_kernel(members, parts, feats_ref, weight_ref, *refs):
    outs, held = refs[:members], refs[members]
    mine = lax.axis_index("member")
    tile = feats_ref.shape[0] // parts
    share = weight_ref.shape[1] // members
    for p in range(parts):
        prod = jnp.dot(
            feats_ref[p * tile : (p + 1) * tile, :], weight_ref[...], preferred_element_type=f32
        )
        held[p] = prod.T * (1.0 / members)
    for k in range(members):
        other = lax.rem(mine + k, members)
        first = pl.multiple_of(other * share, share)
        for p in range(parts):
            outs[k][p] = held[p, pl.ds(first, share), :].astype(outs[k].dtype)


def project(feats, weight, parts):
    members = lax.axis_size("member")
    nodes, _ = feats.shape
    classes = weight.shape[1]
    tile = nodes // parts
    share = classes // members
    return pl.pallas_call(
        functools.partial(project_kernel, members, parts),
        out_shape=[jax.ShapeDtypeStruct((parts, share, tile), bf16)] * members,
        in_specs=[vmem, vmem],
        out_specs=[vmem] * members,
        scratch_shapes=[pltpu.VMEM((parts, classes, tile), f32)],
        name="project",
    )(feats, weight)


def tile_kernel(axis_in, axis_out, n_in, n_out, parts, contract, row_tiles,
                put_ref, pick_ref, count_ref, *refs):
    blocks = refs[:n_in]
    tiles_ref = refs[n_in]
    outs = refs[n_in + 1 : n_in + 1 + n_out]
    source, total = refs[n_in + 1 + n_out :]
    step = pl.program_id(0)
    count = count_ref[0]

    @pl.when(step == 0)
    def _():
        mine = lax.axis_index(axis_in)
        for k in range(n_in):
            owner = lax.rem(mine - k + n_in, n_in)
            source[pl.ds(owner * parts, parts)] = blocks[k][...]
        total[...] = jnp.zeros_like(total)

    first = step * block_tiles

    @pl.when(first < count)
    def _():
        @pl.loop(0, block_tiles // unroll)
        def _(group):
            for u in range(unroll):
                local = group * unroll + u
                slot = first + local
                put = jnp.where(slot < count, put_ref[slot], row_tiles)
                prod = lax.dot_general(
                    source[pick_ref[slot]],
                    tiles_ref[local],
                    (((1,), (contract,)), ((), ())),
                    preferred_element_type=f32,
                )
                total[put] += prod

    @pl.when(step == pl.num_programs(0) - 1)
    def _():
        mine = lax.axis_index(axis_out)
        for k in range(n_out):
            owner = lax.rem(mine + k, n_out)
            outs[k][...] = total[pl.ds(owner * parts, parts)].astype(outs[k].dtype)


def tile_pass(name, blocks, slot_values, put, pick, count, axis_in, axis_out, contract):
    n_in, n_out = lax.axis_size(axis_in), lax.axis_size(axis_out)
    parts, share, tile = blocks[0].shape
    slots = slot_values.shape[0]
    steps = slots // block_tiles
    return pl.pallas_call(
        functools.partial(
            tile_kernel, axis_in, axis_out, n_in, n_out, parts, contract, n_out * parts
        ),
        grid=(steps,),
        out_shape=[jax.ShapeDtypeStruct((parts, share, tile), bf16)] * n_out,
        in_specs=[smem, smem, smem]
        + [vmem] * n_in
        + [pl.BlockSpec((block_tiles, tile, tile), lambda s: (s, 0, 0))],
        out_specs=[vmem] * n_out,
        scratch_shapes=[
            pltpu.VMEM((n_in * parts, share, tile), bf16),
            pltpu.VMEM((n_out * parts + 1, share, tile), f32),
        ],
        cost_estimate=pl.CostEstimate(
            flops=2 * slots * tile * tile * share,
            bytes_accessed=slots * tile * tile * 2,
            transcendentals=0,
        ),
        name=name,
    )(put, pick, count, *blocks, slot_values)


def finish_kernel(members, parts, feats_ref, weight_ref, *refs):
    grads = refs[:members]
    input_ref, part_ref, held = refs[members:]
    mine = lax.axis_index("member")
    _, share, tile = grads[0].shape
    for k in range(members):
        owner = lax.rem(mine - k + members, members)
        first = pl.multiple_of(owner * share, share)
        for p in range(parts):
            held[p, pl.ds(first, share), :] = grads[k][p]
    total = None
    for p in range(parts):
        back = held[p]
        prod = jnp.dot(weight_ref[...], back, preferred_element_type=f32)
        input_ref[p * tile : (p + 1) * tile, :] = prod.T.astype(input_ref.dtype)
        term = jnp.dot(back, feats_ref[p * tile : (p + 1) * tile, :], preferred_element_type=f32)
        total = term if total is None else total + term
    total = total.T
    lanes = part_ref.shape[2]
    for h in range(total.shape[1] // lanes):
        piece = total[:, h * lanes : (h + 1) * lanes]
        rows = piece.shape[0] // 8
        part_ref[h * rows : (h + 1) * rows] = piece.reshape(rows, 8, lanes)


def finish(feats, weight, grads):
    members = len(grads)
    parts, share, tile = grads[0].shape
    features, classes = weight.shape
    pieces = features * classes // 1024
    return pl.pallas_call(
        functools.partial(finish_kernel, members, parts),
        out_shape=[
            jax.ShapeDtypeStruct(feats.shape, bf16),
            jax.ShapeDtypeStruct((pieces, 8, 128), f32),
        ],
        in_specs=[vmem] * (2 + members),
        out_specs=[vmem, vmem],
        scratch_shapes=[pltpu.VMEM((parts, classes, tile), bf16)],
        name="finish",
    )(feats, weight, *grads)


def turn_kernel(members, parts, *refs):
    pieces = refs[:members]
    out_ref, held = refs[members:]
    mine = lax.axis_index("member")
    _, share, tile = pieces[0].shape
    for k in range(members):
        owner = lax.rem(mine - k + members, members)
        first = pl.multiple_of(owner * share, share)
        for p in range(parts):
            held[p, pl.ds(first, share), :] = pieces[k][p]
    for p in range(parts):
        out_ref[p * tile : (p + 1) * tile, :] = held[p].T


def turn(pieces):
    members = len(pieces)
    parts, share, tile = pieces[0].shape
    return pl.pallas_call(
        functools.partial(turn_kernel, members, parts),
        out_shape=jax.ShapeDtypeStruct((parts * tile, members * share), f32),
        in_specs=[vmem] * members,
        out_specs=vmem,
        scratch_shapes=[pltpu.VMEM((parts, members * share, tile), f32)],
        name="turn",
    )(*pieces)


def add_up(blocks):
    total = blocks[0].astype(f32)
    for block in blocks[1:]:
        total = total + block.astype(f32)
    return total


def per_device(features, weights, tile_values, tile_rows, tile_cols, tile_counts, labels):
    row_count = lax.axis_size("row")
    rep_count = lax.axis_size("rep")
    feats = features[0]
    weight = weights[0]
    slot_values = tile_values[0, 0]
    slot_rows = tile_rows[0, 0]
    slot_cols = tile_cols[0, 0]
    count = tile_counts[0]
    tile = slot_values.shape[1]
    nodes = feats.shape[0]
    parts = nodes // tile
    all_nodes = nodes * row_count * rep_count

    mixed = exchange_relative(project(feats, weight, parts), "member")
    mixed = add_up(mixed).astype(bf16)
    panel = gather_relative(mixed, "row")
    sums = tile_pass(
        "forward_tiles", panel, slot_values, slot_rows, slot_cols, count, "row", "rep", 1
    )
    logits = add_up(exchange_relative(sums, "rep"))
    share = logits.shape[1]
    own_labels = lax.dynamic_slice_in_dim(labels, lax.axis_index("rep") * nodes, nodes, 0)
    own_labels = own_labels.reshape(parts, 1, tile)
    class_ids = lax.axis_index("member") * share + jnp.arange(share, dtype=jnp.int32)
    targets = (own_labels == class_ids[None, :, None]).astype(f32)
    grads = (jax.nn.sigmoid(logits) - targets).astype(bf16)
    grad_blocks = gather_relative(grads, "rep")
    logits, *grad_blocks = lax.optimization_barrier((logits, *grad_blocks))
    logit_pieces = gather_relative(logits, "member")
    back = tile_pass(
        "backward_tiles", grad_blocks, slot_values, slot_cols, slot_rows, count, "rep", "row", 0
    )
    mean_logits = turn(logit_pieces)
    back = add_up(exchange_relative(back, "row")).astype(bf16)
    input_grad, part = finish(feats, weight, gather_relative(back, "member"))
    part = lax.all_to_all(part, ("row", "rep"), 0, 0)
    piece = jnp.sum(part, axis=0) * (1.0 / math.sqrt(all_nodes))
    spread = lax.all_to_all(
        jnp.broadcast_to(piece[None], part.shape), ("row", "rep"), 0, 0
    )
    features_in, classes = weight.shape
    weight_grad = spread.reshape(classes // 128, features_in // 8, 8, 128)
    weight_grad = weight_grad.transpose(1, 2, 0, 3).reshape(features_in, classes)
    return (mean_logits, weight_grad[None], input_grad[None])


def solution(mesh):
    return jax.shard_map(
        per_device,
        mesh=mesh,
        in_specs=(
            P("member", ("row", "rep"), None),
            P("member", None, None),
            P("row", "rep", None, None, None),
            P("row", "rep", None),
            P("row", "rep", None),
            P("row", "rep"),
            P("row"),
        ),
        out_specs=(
            P(("row", "rep"), None),
            P("member", None, None),
            P("member", ("row", "rep"), None),
        ),
        check_vma=False,
    )
```

```python
import functools
import math

import jax
import jax.numpy as jnp
from jax import lax
from jax.experimental import pallas as pl
from jax.experimental.pallas import tpu as pltpu
from jax.sharding import PartitionSpec as P


bf16 = jnp.bfloat16
f32 = jnp.float32
vmem = pl.BlockSpec(memory_space=pltpu.VMEM)
smem = pl.BlockSpec(memory_space=pltpu.SMEM)

unroll = 8
small_grant = pltpu.CompilerParams(vmem_limit_bytes=6 << 20)
tile_grant = pltpu.CompilerParams(vmem_limit_bytes=8 << 20)


def shift(value, axis, step):
    size = lax.axis_size(axis)
    return lax.ppermute(value, axis, [(j, (j + step) % size) for j in range(size)])


def gather_relative(value, axis):
    size = lax.axis_size(axis)
    return [value] + [shift(value, axis, k) for k in range(1, size)]


def exchange_relative(blocks, axis):
    return [blocks[0]] + [shift(blocks[k], axis, k) for k in range(1, len(blocks))]


def project_kernel(members, parts, feats_ref, weight_ref, *refs):
    outs, held = refs[:members], refs[members]
    mine = lax.axis_index("member")
    tile = feats_ref.shape[0] // parts
    share = weight_ref.shape[1] // members
    for p in range(parts):
        prod = jnp.dot(
            feats_ref[p * tile : (p + 1) * tile, :], weight_ref[...], preferred_element_type=f32
        )
        held[p] = prod.T * (1.0 / members)
    for k in range(members):
        other = lax.rem(mine + k, members)
        first = pl.multiple_of(other * share, share)
        for p in range(parts):
            outs[k][p] = held[p, pl.ds(first, share), :].astype(outs[k].dtype)


def project(feats, weight, parts):
    members = lax.axis_size("member")
    nodes, _ = feats.shape
    classes = weight.shape[1]
    tile = nodes // parts
    share = classes // members
    return pl.pallas_call(
        functools.partial(project_kernel, members, parts),
        out_shape=[jax.ShapeDtypeStruct((parts, share, tile), bf16)] * members,
        in_specs=[vmem, vmem],
        out_specs=[vmem] * members,
        scratch_shapes=[pltpu.VMEM((parts, classes, tile), f32)],
        compiler_params=small_grant,
        name="project",
    )(feats, weight)


def add_tile(contract, slot, count, put_ref, pick_ref, source, tiles_ref, total):
    put = jnp.where(slot < count, put_ref[slot], total.shape[0] - 1)
    prod = lax.dot_general(
        source[pick_ref[slot]],
        tiles_ref[slot],
        (((1,), (contract,)), ((), ())),
        preferred_element_type=f32,
    )
    total[put] += prod


def tile_kernel(contract, put_ref, pick_ref, count_ref, source, tiles_ref, out_ref, total):
    count = count_ref[0]
    total[...] = jnp.zeros_like(total)

    @pl.loop(0, (count + unroll - 1) // unroll)
    def _(group):
        for u in range(unroll):
            slot = group * unroll + u
            add_tile(contract, slot, count, put_ref, pick_ref, source, tiles_ref, total)

    out_ref[...] = total[:-1].astype(out_ref.dtype)


def tile_pass(name, source, slot_values, put, pick, count, out_tiles, contract):
    _, share, tile = source.shape
    slots = slot_values.shape[0]
    scratch = [pltpu.VMEM((out_tiles + 1, share, tile), f32)]
    return pl.pallas_call(
        functools.partial(tile_kernel, contract),
        out_shape=jax.ShapeDtypeStruct((out_tiles, share, tile), bf16),
        in_specs=[smem, smem, smem, vmem, vmem],
        out_specs=vmem,
        scratch_shapes=scratch,
        cost_estimate=pl.CostEstimate(
            flops=2 * slots * tile * tile * share,
            bytes_accessed=slots * tile * tile * 2,
            transcendentals=0,
        ),
        compiler_params=tile_grant,
        name=name,
    )(put, pick, count, source, slot_values)


def finish_kernel(members, parts, feats_ref, weight_ref, *refs):
    grads = refs[:members]
    input_ref, part_ref, held = refs[members:]
    mine = lax.axis_index("member")
    _, share, tile = grads[0].shape
    for k in range(members):
        owner = lax.rem(mine - k + members, members)
        first = pl.multiple_of(owner * share, share)
        for p in range(parts):
            held[p, pl.ds(first, share), :] = grads[k][p]
    total = None
    for p in range(parts):
        back = held[p]
        prod = jnp.dot(weight_ref[...], back, preferred_element_type=f32)
        input_ref[p * tile : (p + 1) * tile, :] = prod.T.astype(input_ref.dtype)
        term = jnp.dot(back, feats_ref[p * tile : (p + 1) * tile, :], preferred_element_type=f32)
        total = term if total is None else total + term
    total = total.T
    lanes = part_ref.shape[2]
    for h in range(total.shape[1] // lanes):
        piece = total[:, h * lanes : (h + 1) * lanes]
        rows = piece.shape[0] // 8
        part_ref[h * rows : (h + 1) * rows] = piece.reshape(rows, 8, lanes).astype(part_ref.dtype)


def finish(feats, weight, grads):
    members = len(grads)
    parts, share, tile = grads[0].shape
    features, classes = weight.shape
    pieces = features * classes // 1024
    return pl.pallas_call(
        functools.partial(finish_kernel, members, parts),
        out_shape=[
            jax.ShapeDtypeStruct(feats.shape, bf16),
            jax.ShapeDtypeStruct((pieces, 8, 128), bf16),
        ],
        in_specs=[vmem] * (2 + members),
        out_specs=[vmem, vmem],
        scratch_shapes=[pltpu.VMEM((parts, classes, tile), bf16)],
        compiler_params=small_grant,
        name="finish",
    )(feats, weight, *grads)


def turn_kernel(members, parts, *refs):
    pieces = refs[:members]
    out_ref, held = refs[members:]
    mine = lax.axis_index("member")
    _, share, tile = pieces[0].shape
    for k in range(members):
        owner = lax.rem(mine - k + members, members)
        first = pl.multiple_of(owner * share, share)
        for p in range(parts):
            held[p, pl.ds(first, share), :] = pieces[k][p]
    for p in range(parts):
        out_ref[p * tile : (p + 1) * tile, :] = held[p].T


def turn(pieces):
    members = len(pieces)
    parts, share, tile = pieces[0].shape
    return pl.pallas_call(
        functools.partial(turn_kernel, members, parts),
        out_shape=jax.ShapeDtypeStruct((parts * tile, members * share), f32),
        in_specs=[vmem] * members,
        out_specs=vmem,
        scratch_shapes=[pltpu.VMEM((parts, members * share, tile), f32)],
        compiler_params=small_grant,
        name="turn",
    )(*pieces)


def gather_whole(value, axis):
    size = lax.axis_size(axis)
    return lax.all_to_all(jnp.broadcast_to(value[None], (size, *value.shape)), axis, 0, 0)


def exchange_far(blocks, axis):
    size = lax.axis_size(axis)
    mine = lax.axis_index(axis)
    half = size // 2
    order = [half]
    for k in range(half - 1, 0, -1):
        order += [k, size - k]
    parts = [lax.dynamic_index_in_dim(blocks, mine, 0, keepdims=False)]
    for k in order:
        block = lax.dynamic_index_in_dim(blocks, lax.rem(mine + k, size), 0, keepdims=False)
        parts.append(shift(block, axis, k))
    return parts


def add_up(blocks):
    total = blocks[0].astype(f32)
    for block in blocks[1:]:
        total = total + block.astype(f32)
    return total


def per_device(features, weights, tile_values, tile_rows, tile_cols, tile_counts, labels):
    row_count = lax.axis_size("row")
    rep_count = lax.axis_size("rep")
    feats = features[0]
    weight = weights[0]
    slot_values = tile_values[0, 0]
    slot_rows = tile_rows[0, 0]
    slot_cols = tile_cols[0, 0]
    count = tile_counts[0]
    tile = slot_values.shape[1]
    nodes = feats.shape[0]
    parts = nodes // tile
    all_nodes = nodes * row_count * rep_count

    mixed = exchange_relative(project(feats, weight, parts), "member")
    mixed = add_up(mixed).astype(bf16)
    panel = gather_whole(mixed, "row").reshape(row_count * parts, -1, tile)
    sums = tile_pass(
        "forward_tiles", panel, slot_values, slot_rows, slot_cols, count, rep_count * parts, 1
    )
    sums = sums.reshape(rep_count, parts, -1, tile)
    logits = add_up(exchange_far(sums, "rep"))
    share = logits.shape[1]
    own_labels = lax.dynamic_slice_in_dim(labels, lax.axis_index("rep") * nodes, nodes, 0)
    own_labels = own_labels.reshape(parts, 1, tile)
    class_ids = lax.axis_index("member") * share + jnp.arange(share, dtype=jnp.int32)
    targets = (own_labels == class_ids[None, :, None]).astype(f32)
    grads = (jax.nn.sigmoid(logits) - targets).astype(bf16)
    grad_blocks = gather_whole(grads, "rep")
    logits, grad_blocks = lax.optimization_barrier((logits, grad_blocks))
    logit_pieces = gather_relative(logits, "member")
    back = tile_pass(
        "backward_tiles",
        grad_blocks.reshape(rep_count * parts, -1, tile),
        slot_values,
        slot_cols,
        slot_rows,
        count,
        row_count * parts,
        0,
    )
    mean_logits = turn(logit_pieces)
    back = lax.all_to_all(back.reshape(row_count, parts, -1, tile), "row", 0, 0)
    back = jnp.sum(back.astype(f32), axis=0).astype(bf16)
    input_grad, part = finish(feats, weight, gather_relative(back, "member"))
    part = lax.all_to_all(part, ("row", "rep"), 0, 0)
    piece = jnp.sum(part.astype(f32), axis=0) * (1.0 / math.sqrt(all_nodes))
    spread = lax.all_to_all(
        jnp.broadcast_to(piece[None], part.shape), ("row", "rep"), 0, 0
    )
    features_in, classes = weight.shape
    weight_grad = spread.reshape(classes // 128, features_in // 8, 8, 128)
    weight_grad = weight_grad.transpose(1, 2, 0, 3).reshape(features_in, classes)
    return (mean_logits, weight_grad[None], input_grad[None])


def solution(mesh):
    return jax.shard_map(
        per_device,
        mesh=mesh,
        in_specs=(
            P("member", ("row", "rep"), None),
            P("member", None, None),
            P("row", "rep", None, None, None),
            P("row", "rep", None),
            P("row", "rep", None),
            P("row", "rep"),
            P("row"),
        ),
        out_specs=(
            P(("row", "rep"), None),
            P("member", None, None),
            P("member", ("row", "rep"), None),
        ),
        check_vma=False,
    )
```

```python
import functools
import math

import jax
import jax.numpy as jnp
from jax import lax
from jax.experimental import pallas as pl
from jax.experimental.pallas import tpu as pltpu
from jax.sharding import PartitionSpec as P


bf16 = jnp.bfloat16
f32 = jnp.float32
vmem = pl.BlockSpec(memory_space=pltpu.VMEM)
smem = pl.BlockSpec(memory_space=pltpu.SMEM)

unroll = 64
flip_chunks = 16
small_grant = pltpu.CompilerParams(vmem_limit_bytes=6 << 20)
flip_grant = pltpu.CompilerParams(vmem_limit_bytes=40 << 20)
tile_grant = pltpu.CompilerParams(vmem_limit_bytes=8 << 20)


def shift(value, axis, step):
    size = lax.axis_size(axis)
    return lax.ppermute(value, axis, [(j, (j + step) % size) for j in range(size)])


def gather_relative(value, axis):
    size = lax.axis_size(axis)
    return [value] + [shift(value, axis, k) for k in range(1, size)]


def exchange_relative(blocks, axis):
    return [blocks[0]] + [shift(blocks[k], axis, k) for k in range(1, len(blocks))]


def project_kernel(members, parts, feats_ref, weight_ref, *refs):
    outs, held = refs[:members], refs[members]
    mine = lax.axis_index("member")
    tile = feats_ref.shape[0] // parts
    share = weight_ref.shape[1] // members
    for p in range(parts):
        prod = jnp.dot(
            feats_ref[p * tile : (p + 1) * tile, :], weight_ref[...], preferred_element_type=f32
        )
        held[p] = prod.T * (1.0 / members)
    for k in range(members):
        other = lax.rem(mine + k, members)
        first = pl.multiple_of(other * share, share)
        for p in range(parts):
            outs[k][p] = held[p, pl.ds(first, share), :].astype(outs[k].dtype)


def project(feats, weight, parts):
    members = lax.axis_size("member")
    nodes, _ = feats.shape
    classes = weight.shape[1]
    tile = nodes // parts
    share = classes // members
    return pl.pallas_call(
        functools.partial(project_kernel, members, parts),
        out_shape=[jax.ShapeDtypeStruct((parts, share, tile), bf16)] * members,
        in_specs=[vmem, vmem],
        out_specs=[vmem] * members,
        scratch_shapes=[pltpu.VMEM((parts, classes, tile), f32)],
        compiler_params=small_grant,
        name="project",
    )(feats, weight)


def flip_kernel(stored, out_ref, held, sems):
    chunks = sems.shape[0]
    size = stored.shape[0] // chunks

    def load(chunk):
        part = pl.ds(chunk * size, size)
        return pltpu.make_async_copy(stored.at[part], held.at[part], sems.at[chunk])

    for chunk in range(chunks):
        load(chunk).start()

    @pl.loop(0, chunks)
    def _(chunk):
        load(chunk).wait()
        for k in range(size):
            slot = chunk * size + k
            out_ref[slot] = held[slot].T


def flip(slot_values):
    slots, tile, _ = slot_values.shape
    return pl.pallas_call(
        flip_kernel,
        out_shape=jax.ShapeDtypeStruct(slot_values.shape, bf16),
        in_specs=[pl.BlockSpec(memory_space=pl.ANY)],
        out_specs=vmem,
        scratch_shapes=[
            pltpu.VMEM(slot_values.shape, bf16),
            pltpu.SemaphoreType.DMA((flip_chunks,)),
        ],
        cost_estimate=pl.CostEstimate(
            flops=0, bytes_accessed=4 * slots * tile * tile, transcendentals=0
        ),
        compiler_params=flip_grant,
        name="flip",
    )(slot_values)


def tile_kernel(axis_in, axis_out, n_in, n_out, places_ref, count_ref, *refs):
    blocks, tiles_ref, outs = refs[:n_in], refs[n_in], refs[n_in + 1 : n_in + 1 + n_out]
    source, total = refs[n_in + 1 + n_out :]
    parts = blocks[0].shape[0]
    mine = lax.axis_index(axis_in)
    for k in range(n_in):
        owner = lax.rem(mine - k + n_in, n_in)
        source[pl.ds(owner * parts, parts)] = blocks[k][...]
    total[...] = jnp.zeros_like(total)

    @pl.loop(0, (count_ref[0, 0] + unroll - 1) // unroll)
    def _(group):
        for u in range(unroll):
            slot = group * unroll + u
            total[places_ref[0, slot]] += jnp.dot(
                source[places_ref[1, slot]], tiles_ref[slot], preferred_element_type=f32
            )

    size = outs[0].shape[0]
    mine = lax.axis_index(axis_out)
    for k in range(n_out):
        owner = lax.rem(mine + k, n_out)
        outs[k][...] = total[pl.ds(owner * size, size)].astype(outs[k].dtype)


def tile_pass(name, blocks, axis_in, axis_out, tiles, places, count, out_tiles, n_out):
    n_in = len(blocks)
    parts, share, tile = blocks[0].shape
    slots = tiles.shape[0]
    return pl.pallas_call(
        functools.partial(tile_kernel, axis_in, axis_out, n_in, n_out),
        out_shape=[jax.ShapeDtypeStruct((out_tiles // n_out, share, tile), bf16)] * n_out,
        in_specs=[smem, smem] + [vmem] * (n_in + 1),
        out_specs=[vmem] * n_out,
        scratch_shapes=[
            pltpu.VMEM((parts * n_in, share, tile), bf16),
            pltpu.VMEM((out_tiles + 1, share, tile), f32),
        ],
        cost_estimate=pl.CostEstimate(
            flops=2 * slots * tile * tile * share,
            bytes_accessed=slots * tile * tile * 2,
            transcendentals=0,
        ),
        compiler_params=tile_grant,
        name=name,
    )(places, count, *blocks, tiles)


def grade_kernel(n_in, labels_ref, *refs):
    blocks, (logits_ref, grads_ref) = refs[:n_in], refs[n_in:]
    parts, share, tile = logits_ref.shape
    first = lax.axis_index("rep") * parts
    classes = lax.broadcasted_iota(jnp.int32, (share, tile), 0) + lax.axis_index("member") * share
    for p in range(parts):
        logits = add_up([block[p] for block in blocks])
        logits_ref[p] = logits
        target = labels_ref[pl.ds(first + p, 1), :] == classes
        grads_ref[p] = (jax.nn.sigmoid(logits) - target.astype(f32)).astype(grads_ref.dtype)


def grade(labels, blocks):
    shape = blocks[0].shape
    return pl.pallas_call(
        functools.partial(grade_kernel, len(blocks)),
        out_shape=[jax.ShapeDtypeStruct(shape, f32), jax.ShapeDtypeStruct(shape, bf16)],
        in_specs=[vmem] * (len(blocks) + 1),
        out_specs=[vmem, vmem],
        compiler_params=small_grant,
        name="grade",
    )(labels.reshape(-1, shape[2]), *blocks)


def finish_kernel(members, parts, feats_ref, weight_ref, *refs):
    grads = refs[:members]
    input_ref, part_ref, held = refs[members:]
    mine = lax.axis_index("member")
    _, share, tile = grads[0].shape
    for k in range(members):
        owner = lax.rem(mine - k + members, members)
        first = pl.multiple_of(owner * share, share)
        for p in range(parts):
            held[p, pl.ds(first, share), :] = grads[k][p]
    total = None
    for p in range(parts):
        back = held[p]
        prod = jnp.dot(weight_ref[...], back, preferred_element_type=f32)
        input_ref[p * tile : (p + 1) * tile, :] = prod.T.astype(input_ref.dtype)
        term = jnp.dot(back, feats_ref[p * tile : (p + 1) * tile, :], preferred_element_type=f32)
        total = term if total is None else total + term
    total = total.T
    _, halves, _, lanes = part_ref.shape
    for h in range(halves):
        piece = total[:, h * lanes : (h + 1) * lanes].astype(part_ref.dtype)
        part_ref[:, h] = piece.reshape(-1, 8, lanes)


def finish(feats, weight, grads):
    members = len(grads)
    parts, share, tile = grads[0].shape
    features, classes = weight.shape
    return pl.pallas_call(
        functools.partial(finish_kernel, members, parts),
        out_shape=[
            jax.ShapeDtypeStruct(feats.shape, bf16),
            jax.ShapeDtypeStruct((features // 8, classes // 128, 8, 128), bf16),
        ],
        in_specs=[vmem] * (2 + members),
        out_specs=[vmem, vmem],
        scratch_shapes=[pltpu.VMEM((parts, classes, tile), bf16)],
        compiler_params=small_grant,
        name="finish",
    )(feats, weight, *grads)


def turn_kernel(members, parts, *refs):
    pieces = refs[:members]
    out_ref, held = refs[members:]
    mine = lax.axis_index("member")
    _, share, tile = pieces[0].shape
    for k in range(members):
        owner = lax.rem(mine - k + members, members)
        first = pl.multiple_of(owner * share, share)
        for p in range(parts):
            held[p, pl.ds(first, share), :] = pieces[k][p]
    for p in range(parts):
        out_ref[p * tile : (p + 1) * tile, :] = held[p].T


def turn(pieces):
    members = len(pieces)
    parts, share, tile = pieces[0].shape
    return pl.pallas_call(
        functools.partial(turn_kernel, members, parts),
        out_shape=jax.ShapeDtypeStruct((parts * tile, members * share), f32),
        in_specs=[vmem] * members,
        out_specs=vmem,
        scratch_shapes=[pltpu.VMEM((parts, members * share, tile), f32)],
        compiler_params=small_grant,
        name="turn",
    )(*pieces)


def far_first(size):
    half = size // 2
    return [half] + [k for j in range(half - 1, 0, -1) for k in (j, size - j)]


def gather_far(value, axis):
    size = lax.axis_size(axis)
    parts = {k: shift(value, axis, k) for k in far_first(size)}
    return [value] + [parts[k] for k in range(1, size)]


def exchange_far(blocks, axis):
    return [blocks[0]] + [shift(blocks[k], axis, k) for k in far_first(len(blocks))]


def add_up(blocks):
    total = blocks[0].astype(f32)
    for block in blocks[1:]:
        total = total + block.astype(f32)
    return total


def per_device(features, weights, tile_values, tile_rows, tile_cols, tile_counts, labels):
    row_count = lax.axis_size("row")
    rep_count = lax.axis_size("rep")
    feats = features[0]
    weight = weights[0]
    slot_values = tile_values[0, 0]
    slot_rows = tile_rows[0, 0]
    slot_cols = tile_cols[0, 0]
    count = tile_counts
    tile = slot_values.shape[1]
    nodes = feats.shape[0]
    parts = nodes // tile
    all_nodes = nodes * row_count * rep_count

    mixed = exchange_relative(project(feats, weight, parts), "member")
    mixed = add_up(mixed).astype(bf16)
    mixed, later_values = lax.optimization_barrier((mixed, slot_values))
    panel = gather_far(mixed, "row")
    live = jnp.arange(slot_rows.shape[0], dtype=jnp.int32) < count[0, 0]
    to_rows = jnp.stack([jnp.where(live, slot_rows, rep_count * parts), slot_cols])
    to_cols = jnp.stack([jnp.where(live, slot_cols, row_count * parts), slot_rows])
    sums = tile_pass(
        "forward_tiles",
        panel,
        "row",
        "rep",
        flip(later_values),
        to_rows,
        count,
        rep_count * parts,
        rep_count,
    )
    logits, grads = grade(labels, exchange_far(sums, "rep"))
    grad_blocks = gather_far(grads, "rep")
    logits, *grad_blocks = lax.optimization_barrier((logits, *grad_blocks))
    logit_pieces = gather_relative(logits, "member")
    (back,) = tile_pass(
        "backward_tiles",
        grad_blocks,
        "rep",
        "row",
        slot_values,
        to_cols,
        count,
        row_count * parts,
        1,
    )
    mean_logits = turn(logit_pieces)
    back = lax.all_to_all(back.reshape(row_count, parts, -1, tile), "row", 0, 0)
    back = jnp.sum(back.astype(f32), axis=0).astype(bf16)
    input_grad, part = finish(feats, weight, gather_relative(back, "member"))
    part = lax.all_to_all(part.reshape(-1, 8, 128), ("row", "rep"), 0, 0)
    piece = (jnp.sum(part.astype(f32), axis=0) * (1.0 / math.sqrt(all_nodes))).astype(bf16)
    spread = lax.all_to_all(jnp.broadcast_to(piece[None], part.shape), ("row", "rep"), 0, 0)
    features_in, classes = weight.shape
    weight_grad = spread.astype(f32).reshape(features_in // 8, classes // 128, 8, 128)
    weight_grad = weight_grad.transpose(0, 2, 1, 3).reshape(features_in, classes)
    return (mean_logits, weight_grad[None], input_grad[None])


def solution(mesh):
    return jax.shard_map(
        per_device,
        mesh=mesh,
        in_specs=(
            P("member", ("row", "rep"), None),
            P("member", None, None),
            P("row", "rep", None, None, None),
            P("row", "rep", None),
            P("row", "rep", None),
            P("row", "rep"),
            P("row"),
        ),
        out_specs=(
            P(("row", "rep"), None),
            P("member", None, None),
            P("member", ("row", "rep"), None),
        ),
        check_vma=False,
    )
```

```python
import functools
import math

import jax
import jax.numpy as jnp
from jax import lax
from jax.experimental import pallas as pl
from jax.experimental.pallas import tpu as pltpu
from jax.sharding import PartitionSpec as P


bf16 = jnp.bfloat16
f32 = jnp.float32
vmem = pl.BlockSpec(memory_space=pltpu.VMEM)
smem = pl.BlockSpec(memory_space=pltpu.SMEM)

unroll = 64
flip_chunks = 8
small_grant = pltpu.CompilerParams(vmem_limit_bytes=6 << 20)
flip_grant = pltpu.CompilerParams(vmem_limit_bytes=44 << 20)
tile_grant = pltpu.CompilerParams(vmem_limit_bytes=8 << 20)


def shift(value, axis, step):
    size = lax.axis_size(axis)
    return lax.ppermute(value, axis, [(j, (j + step) % size) for j in range(size)])


def gather_relative(value, axis):
    size = lax.axis_size(axis)
    return [value] + [shift(value, axis, k) for k in range(1, size)]


def exchange_relative(blocks, axis):
    return [blocks[0]] + [shift(blocks[k], axis, k) for k in range(1, len(blocks))]


def project_kernel(members, parts, feats_ref, weight_ref, *refs):
    outs, held = refs[:members], refs[members]
    mine = lax.axis_index("member")
    tile = feats_ref.shape[0] // parts
    share = weight_ref.shape[1] // members
    for p in range(parts):
        prod = jnp.dot(
            feats_ref[p * tile : (p + 1) * tile, :], weight_ref[...], preferred_element_type=f32
        )
        held[p] = prod.T * (1.0 / members)
    for k in range(members):
        other = lax.rem(mine + k, members)
        first = pl.multiple_of(other * share, share)
        for p in range(parts):
            outs[k][p] = held[p, pl.ds(first, share), :].astype(outs[k].dtype)


def project(feats, weight, parts):
    members = lax.axis_size("member")
    nodes, _ = feats.shape
    classes = weight.shape[1]
    tile = nodes // parts
    share = classes // members
    return pl.pallas_call(
        functools.partial(project_kernel, members, parts),
        out_shape=[jax.ShapeDtypeStruct((parts, share, tile), bf16)] * members,
        in_specs=[vmem, vmem],
        out_specs=[vmem] * members,
        scratch_shapes=[pltpu.VMEM((parts, classes, tile), f32)],
        compiler_params=small_grant,
        name="project",
    )(feats, weight)


def flip_kernel(first, stored, out_ref, held, sems):
    chunks = sems.shape[0]
    size = out_ref.shape[0] // chunks

    def load(chunk):
        return pltpu.make_async_copy(
            stored.at[pl.ds(first + chunk * size, size)],
            held.at[pl.ds(chunk * size, size)],
            sems.at[chunk],
        )

    for chunk in range(chunks):
        load(chunk).start()

    @pl.loop(0, chunks)
    def _(chunk):
        load(chunk).wait()
        for k in range(size):
            slot = chunk * size + k
            out_ref[slot] = held[slot].T


def flip(slot_values, part, parts):
    slots, tile, _ = slot_values.shape
    shape = (slots // parts, tile, tile)
    return pl.pallas_call(
        functools.partial(flip_kernel, part * shape[0]),
        out_shape=jax.ShapeDtypeStruct(shape, bf16),
        in_specs=[pl.BlockSpec(memory_space=pl.ANY)],
        out_specs=vmem,
        scratch_shapes=[pltpu.VMEM(shape, bf16), pltpu.SemaphoreType.DMA((flip_chunks,))],
        cost_estimate=pl.CostEstimate(
            flops=0, bytes_accessed=4 * shape[0] * tile * tile, transcendentals=0
        ),
        compiler_params=flip_grant,
        name="flip",
    )(slot_values)


def tile_kernel(
    offsets, n_tiles, n_out, axis_in, axis_out, put_ref, pick_ref, count_ref, *refs
):
    n_in = len(offsets)
    blocks, refs = refs[:n_in], refs[n_in:]
    tile_refs, outs = refs[:n_tiles], refs[n_tiles : n_tiles + n_out]
    source, total = refs[n_tiles + n_out :]
    parts = blocks[0].shape[0]
    last = total.shape[0] - 1
    count = count_ref[0, 0]
    mine = lax.axis_index(axis_in)
    for block, offset in zip(blocks, offsets):
        source[pl.ds(offset(mine) * parts, parts)] = block[...]
    total[...] = jnp.zeros_like(total)
    first = 0
    for tiles_ref in tile_refs:
        slots = tiles_ref.shape[0]
        left = jnp.clip(count - first, 0, slots)

        @pl.loop(0, (left + unroll - 1) // unroll)
        def _(group):
            for u in range(unroll):
                local = group * unroll + u
                slot = first + local
                put = jnp.where(slot < count, put_ref[slot], last)
                total[put] += jnp.dot(
                    source[pick_ref[slot]], tiles_ref[local], preferred_element_type=f32
                )

        first += slots

    size = outs[0].shape[0]
    mine = lax.axis_index(axis_out)
    for k in range(n_out):
        owner = lax.rem(mine + k, n_out)
        outs[k][...] = total[pl.ds(owner * size, size)].astype(outs[k].dtype)


def tile_pass(name, gathered, axis_in, axis_out, tiles, put, pick, count, out_tiles, n_out):
    offsets, blocks = zip(*gathered)
    n_in = len(blocks)
    parts, share, tile = blocks[0].shape
    slots = put.shape[0]
    return pl.pallas_call(
        functools.partial(tile_kernel, offsets, len(tiles), n_out, axis_in, axis_out),
        out_shape=[jax.ShapeDtypeStruct((out_tiles // n_out, share, tile), bf16)] * n_out,
        in_specs=[smem, smem, smem] + [vmem] * (n_in + len(tiles)),
        out_specs=[vmem] * n_out,
        scratch_shapes=[
            pltpu.VMEM((parts * n_in, share, tile), bf16),
            pltpu.VMEM((out_tiles + 1, share, tile), f32),
        ],
        cost_estimate=pl.CostEstimate(
            flops=2 * slots * tile * tile * share,
            bytes_accessed=slots * tile * tile * 2,
            transcendentals=0,
        ),
        compiler_params=tile_grant,
        name=name,
    )(put, pick, count, *blocks, *tiles)


def grade_kernel(n_in, labels_ref, *refs):
    blocks, (logits_ref, grads_ref) = refs[:n_in], refs[n_in:]
    parts, share, tile = logits_ref.shape
    first = lax.axis_index("rep") * parts
    classes = lax.broadcasted_iota(jnp.int32, (share, tile), 0) + lax.axis_index("member") * share
    for p in range(parts):
        logits = add_up([block[p] for block in blocks])
        logits_ref[p] = logits
        target = labels_ref[pl.ds(first + p, 1), :] == classes
        grads_ref[p] = (jax.nn.sigmoid(logits) - target.astype(f32)).astype(grads_ref.dtype)


def grade(labels, blocks):
    shape = blocks[0].shape
    return pl.pallas_call(
        functools.partial(grade_kernel, len(blocks)),
        out_shape=[jax.ShapeDtypeStruct(shape, f32), jax.ShapeDtypeStruct(shape, bf16)],
        in_specs=[vmem] * (len(blocks) + 1),
        out_specs=[vmem, vmem],
        compiler_params=small_grant,
        name="grade",
    )(labels.reshape(-1, shape[2]), *blocks)


def join_members(pieces, held):
    members = len(pieces)
    mine = lax.axis_index("member")
    parts, share, _ = pieces[0].shape
    for k in range(members):
        owner = lax.rem(mine - k + members, members)
        first = pl.multiple_of(owner * share, share)
        for p in range(parts):
            held[p, pl.ds(first, share), :] = pieces[k][p]


def weight_kernel(feats_ref, *refs):
    grads, (part_ref, held) = refs[:-2], refs[-2:]
    parts, _, tile = held.shape
    join_members(grads, held)
    total = None
    for p in range(parts):
        feats = feats_ref[p * tile : (p + 1) * tile, :]
        term = jnp.dot(held[p], feats, preferred_element_type=f32)
        total = term if total is None else total + term
    total = total.T
    _, halves, _, lanes = part_ref.shape
    for h in range(halves):
        piece = total[:, h * lanes : (h + 1) * lanes].astype(part_ref.dtype)
        part_ref[:, h] = piece.reshape(-1, 8, lanes)


def weight_part(feats, grads):
    parts, share, tile = grads[0].shape
    features, classes = feats.shape[1], share * len(grads)
    return pl.pallas_call(
        weight_kernel,
        out_shape=jax.ShapeDtypeStruct((features // 8, classes // 128, 8, 128), bf16),
        in_specs=[vmem] * (1 + len(grads)),
        out_specs=vmem,
        scratch_shapes=[pltpu.VMEM((parts, classes, tile), bf16)],
        compiler_params=small_grant,
        name="weight_part",
    )(feats, *grads)


def input_kernel(weight_ref, *refs):
    grads, (input_ref, held) = refs[:-2], refs[-2:]
    parts, _, tile = held.shape
    join_members(grads, held)
    for p in range(parts):
        prod = jnp.dot(weight_ref[...], held[p], preferred_element_type=f32)
        input_ref[p * tile : (p + 1) * tile, :] = prod.T.astype(input_ref.dtype)


def input_part(weight, grads):
    parts, share, tile = grads[0].shape
    features, classes = weight.shape
    return pl.pallas_call(
        input_kernel,
        out_shape=jax.ShapeDtypeStruct((parts * tile, features), bf16),
        in_specs=[vmem] * (1 + len(grads)),
        out_specs=vmem,
        scratch_shapes=[pltpu.VMEM((parts, classes, tile), bf16)],
        compiler_params=small_grant,
        name="input_part",
    )(weight, *grads)


def turn_kernel(*refs):
    pieces, (out_ref, held) = refs[:-2], refs[-2:]
    parts, _, tile = held.shape
    join_members(pieces, held)
    for p in range(parts):
        out_ref[p * tile : (p + 1) * tile, :] = held[p].T


def turn(pieces):
    members = len(pieces)
    parts, share, tile = pieces[0].shape
    return pl.pallas_call(
        turn_kernel,
        out_shape=jax.ShapeDtypeStruct((parts * tile, members * share), f32),
        in_specs=[vmem] * members,
        out_specs=vmem,
        scratch_shapes=[pltpu.VMEM((parts, members * share, tile), f32)],
        compiler_params=small_grant,
        name="turn",
    )(*pieces)


def far_first(size):
    half = size // 2
    return [half] + [k for j in range(half - 1, 0, -1) for k in (j, size - j)]


def gather_far(value, axis):
    size = lax.axis_size(axis)
    found = [(lambda mine: mine, value)]
    for k in far_first(size):
        found.append((lambda mine, k=k: lax.rem(mine - k + size, size), shift(value, axis, k)))
    return found


def gather_pairs(value, axis):
    size = lax.axis_size(axis)
    half = size // 2

    def partner(r):
        return r + 1 - 2 * lax.rem(r, 2)

    def turned(r, k):
        return lax.rem(r + 2 * (half - k), size)

    def send(block, k):
        return lax.ppermute(block, axis, [(r, (r + 2 * k) % size) for r in range(size)])

    other = lax.ppermute(value, axis, [(r, r ^ 1) for r in range(size)])
    order = sorted(range(1, half), key=lambda k: -min(k, half - k))
    found = [(lambda mine: mine, value), (partner, other)]
    for block, where in ((value, lambda r: r), (other, partner)):
        for k in order:
            place = lambda mine, k=k, where=where: where(turned(mine, k))
            found.append((place, send(block, k)))
    return found


def exchange_far(blocks, axis):
    return [blocks[0]] + [shift(blocks[k], axis, k) for k in far_first(len(blocks))]


def add_up(blocks):
    total = blocks[0].astype(f32)
    for block in blocks[1:]:
        total = total + block.astype(f32)
    return total


def per_device(features, weights, tile_values, tile_rows, tile_cols, tile_counts, labels):
    row_count = lax.axis_size("row")
    rep_count = lax.axis_size("rep")
    feats = features[0]
    weight = weights[0]
    slot_values = tile_values[0, 0]
    slot_rows = tile_rows[0, 0]
    slot_cols = tile_cols[0, 0]
    count = tile_counts
    tile = slot_values.shape[1]
    nodes = feats.shape[0]
    parts = nodes // tile
    all_nodes = nodes * row_count * rep_count

    mixed = exchange_relative(project(feats, weight, parts), "member")
    mixed = add_up(mixed).astype(bf16)
    early = flip(slot_values, 0, 2)
    mixed, early, later_values = lax.optimization_barrier((mixed, early, slot_values))
    panel = gather_pairs(mixed, "row")
    sums = tile_pass(
        "forward_tiles",
        panel,
        "row",
        "rep",
        [early, flip(later_values, 1, 2)],
        slot_rows,
        slot_cols,
        count,
        rep_count * parts,
        rep_count,
    )
    logits, grads = grade(labels, exchange_far(sums, "rep"))
    (back,) = tile_pass(
        "backward_tiles",
        gather_far(grads, "rep"),
        "rep",
        "row",
        [slot_values],
        slot_cols,
        slot_rows,
        count,
        row_count * parts,
        1,
    )
    back = lax.all_to_all(back.reshape(row_count, parts, -1, tile), "row", 0, 0)
    back = jnp.sum(back.astype(f32), axis=0).astype(bf16)
    back = gather_relative(back, "member")
    part = weight_part(feats, back)
    part = lax.all_to_all(part.reshape(-1, 8, 128), ("row", "rep"), 0, 0)
    piece = (jnp.sum(part.astype(f32), axis=0) * (1.0 / math.sqrt(all_nodes))).astype(bf16)
    piece, logits, *back = lax.optimization_barrier((piece, logits, *back))
    spread = lax.all_to_all(jnp.broadcast_to(piece[None], part.shape), ("row", "rep"), 0, 0)
    mean_logits = turn(gather_relative(logits, "member"))
    input_grad = input_part(weight, back)
    features_in, classes = weight.shape
    weight_grad = spread.astype(f32).reshape(features_in // 8, classes // 128, 8, 128)
    weight_grad = weight_grad.transpose(0, 2, 1, 3).reshape(features_in, classes)
    return (mean_logits, weight_grad[None], input_grad[None])


def solution(mesh):
    return jax.shard_map(
        per_device,
        mesh=mesh,
        in_specs=(
            P("member", ("row", "rep"), None),
            P("member", None, None),
            P("row", "rep", None, None, None),
            P("row", "rep", None),
            P("row", "rep", None),
            P("row", "rep"),
            P("row"),
        ),
        out_specs=(
            P(("row", "rep"), None),
            P("member", None, None),
            P("member", ("row", "rep"), None),
        ),
        check_vma=False,
    )
```

```python
import functools
import math

import jax
import jax.numpy as jnp
from jax import lax
from jax.experimental import pallas as pl
from jax.experimental.pallas import tpu as pltpu
from jax.sharding import PartitionSpec as P


bf16 = jnp.bfloat16
f32 = jnp.float32
vmem = pl.BlockSpec(memory_space=pltpu.VMEM)
smem = pl.BlockSpec(memory_space=pltpu.SMEM)

unroll = 64
flip_chunks = 8
small_grant = pltpu.CompilerParams(vmem_limit_bytes=6 << 20)
flip_grant = pltpu.CompilerParams(vmem_limit_bytes=44 << 20)
tile_grant = pltpu.CompilerParams(vmem_limit_bytes=8 << 20)


def shift(value, axis, step):
    size = lax.axis_size(axis)
    return lax.ppermute(value, axis, [(j, (j + step) % size) for j in range(size)])


def gather_relative(value, axis):
    size = lax.axis_size(axis)
    return [value] + [shift(value, axis, k) for k in range(1, size)]


def exchange_relative(blocks, axis):
    return [blocks[0]] + [shift(blocks[k], axis, k) for k in range(1, len(blocks))]


def project_kernel(members, parts, feats_ref, weight_ref, *refs):
    outs, held = refs[:members], refs[members]
    mine = lax.axis_index("member")
    tile = feats_ref.shape[0] // parts
    share = weight_ref.shape[1] // members
    for p in range(parts):
        prod = jnp.dot(
            feats_ref[p * tile : (p + 1) * tile, :], weight_ref[...], preferred_element_type=f32
        )
        held[p] = prod.T * (1.0 / members)
    for k in range(members):
        other = lax.rem(mine + k, members)
        first = pl.multiple_of(other * share, share)
        for p in range(parts):
            outs[k][p] = held[p, pl.ds(first, share), :].astype(outs[k].dtype)


def project(feats, weight, parts):
    members = lax.axis_size("member")
    nodes, _ = feats.shape
    classes = weight.shape[1]
    tile = nodes // parts
    share = classes // members
    return pl.pallas_call(
        functools.partial(project_kernel, members, parts),
        out_shape=[jax.ShapeDtypeStruct((parts, share, tile), bf16)] * members,
        in_specs=[vmem, vmem],
        out_specs=[vmem] * members,
        scratch_shapes=[pltpu.VMEM((parts, classes, tile), f32)],
        compiler_params=small_grant,
        name="project",
    )(feats, weight)


def flip_kernel(first, stored, out_ref, held, sems):
    chunks = sems.shape[0]
    size = out_ref.shape[0] // chunks

    def load(chunk):
        return pltpu.make_async_copy(
            stored.at[pl.ds(first + chunk * size, size)],
            held.at[pl.ds(chunk * size, size)],
            sems.at[chunk],
        )

    for chunk in range(chunks):
        load(chunk).start()

    @pl.loop(0, chunks)
    def _(chunk):
        load(chunk).wait()
        for k in range(size):
            slot = chunk * size + k
            out_ref[slot] = held[slot].T


def flip(slot_values, first, slots):
    _, tile, _ = slot_values.shape
    shape = (slots, tile, tile)
    return pl.pallas_call(
        functools.partial(flip_kernel, first),
        out_shape=jax.ShapeDtypeStruct(shape, bf16),
        in_specs=[pl.BlockSpec(memory_space=pl.ANY)],
        out_specs=vmem,
        scratch_shapes=[pltpu.VMEM(shape, bf16), pltpu.SemaphoreType.DMA((flip_chunks,))],
        cost_estimate=pl.CostEstimate(
            flops=0, bytes_accessed=4 * shape[0] * tile * tile, transcendentals=0
        ),
        compiler_params=flip_grant,
        name="flip",
    )(slot_values)


def tile_kernel(offsets, axis_in, put_ref, pick_ref, count_ref, *refs):
    n_in = len(offsets)
    blocks, tile_refs, (out_ref, source, total) = refs[:n_in], refs[n_in:-3], refs[-3:]
    parts = blocks[0].shape[0]
    last = total.shape[0] - 1
    count = count_ref[0, 0]
    mine = lax.axis_index(axis_in)
    for block, offset in zip(blocks, offsets):
        source[pl.ds(offset(mine) * parts, parts)] = block[...]
    total[...] = jnp.zeros_like(total)
    first = 0
    for tiles_ref in tile_refs:
        slots = tiles_ref.shape[0]
        left = jnp.clip(count - first, 0, slots)

        @pl.loop(0, (left + unroll - 1) // unroll)
        def _(group):
            for u in range(unroll):
                local = group * unroll + u
                slot = first + local
                put = jnp.where(slot < count, put_ref[slot], last)
                total[put] += jnp.dot(
                    source[pick_ref[slot]], tiles_ref[local], preferred_element_type=f32
                )

        first += slots

    out_ref[...] = total[:-1].astype(out_ref.dtype)


def tile_pass(name, gathered, axis_in, tiles, put, pick, count, out_tiles):
    offsets, blocks = zip(*gathered)
    n_in = len(blocks)
    parts, share, tile = blocks[0].shape
    slots = put.shape[0]
    return pl.pallas_call(
        functools.partial(tile_kernel, offsets, axis_in),
        out_shape=jax.ShapeDtypeStruct((out_tiles, share, tile), bf16),
        in_specs=[smem, smem, smem] + [vmem] * (n_in + len(tiles)),
        out_specs=vmem,
        scratch_shapes=[
            pltpu.VMEM((parts * n_in, share, tile), bf16),
            pltpu.VMEM((out_tiles + 1, share, tile), f32),
        ],
        cost_estimate=pl.CostEstimate(
            flops=2 * slots * tile * tile * share,
            bytes_accessed=slots * tile * tile * 2,
            transcendentals=0,
        ),
        compiler_params=tile_grant,
        name=name,
    )(put, pick, count, *blocks, *tiles)


def grade_kernel(labels_ref, sums_ref, logits_ref, grads_ref):
    parts, share, tile = logits_ref.shape
    first = lax.axis_index("rep") * parts
    classes = lax.broadcasted_iota(jnp.int32, (share, tile), 0) + lax.axis_index("member") * share
    for p in range(parts):
        logits = add_up([sums_ref[k, p] for k in range(sums_ref.shape[0])])
        logits_ref[p] = logits
        target = labels_ref[pl.ds(first + p, 1), :] == classes
        grads_ref[p] = (jax.nn.sigmoid(logits) - target.astype(f32)).astype(grads_ref.dtype)


def grade(labels, sums):
    shape = sums.shape[1:]
    return pl.pallas_call(
        grade_kernel,
        out_shape=[jax.ShapeDtypeStruct(shape, f32), jax.ShapeDtypeStruct(shape, bf16)],
        in_specs=[vmem, vmem],
        out_specs=[vmem, vmem],
        compiler_params=small_grant,
        name="grade",
    )(labels.reshape(-1, shape[2]), sums)


def join_members(pieces, held):
    members = len(pieces)
    mine = lax.axis_index("member")
    parts, share, _ = pieces[0].shape
    for k in range(members):
        owner = lax.rem(mine - k + members, members)
        first = pl.multiple_of(owner * share, share)
        for p in range(parts):
            held[p, pl.ds(first, share), :] = pieces[k][p]


def weight_kernel(feats_ref, *refs):
    grads, (part_ref, held) = refs[:-2], refs[-2:]
    parts, _, tile = held.shape
    join_members(grads, held)
    total = None
    for p in range(parts):
        feats = feats_ref[p * tile : (p + 1) * tile, :]
        term = jnp.dot(held[p], feats, preferred_element_type=f32)
        total = term if total is None else total + term
    total = total.T
    _, halves, _, lanes = part_ref.shape
    for h in range(halves):
        piece = total[:, h * lanes : (h + 1) * lanes].astype(part_ref.dtype)
        part_ref[:, h] = piece.reshape(-1, 8, lanes)


def weight_part(feats, grads):
    parts, share, tile = grads[0].shape
    features, classes = feats.shape[1], share * len(grads)
    return pl.pallas_call(
        weight_kernel,
        out_shape=jax.ShapeDtypeStruct((features // 8, classes // 128, 8, 128), bf16),
        in_specs=[vmem] * (1 + len(grads)),
        out_specs=vmem,
        scratch_shapes=[pltpu.VMEM((parts, classes, tile), bf16)],
        compiler_params=small_grant,
        name="weight_part",
    )(feats, *grads)


def input_kernel(weight_ref, *refs):
    grads, (input_ref, held) = refs[:-2], refs[-2:]
    parts, _, tile = held.shape
    join_members(grads, held)
    for p in range(parts):
        prod = jnp.dot(weight_ref[...], held[p], preferred_element_type=f32)
        input_ref[p * tile : (p + 1) * tile, :] = prod.T.astype(input_ref.dtype)


def input_part(weight, grads):
    parts, share, tile = grads[0].shape
    features, classes = weight.shape
    return pl.pallas_call(
        input_kernel,
        out_shape=jax.ShapeDtypeStruct((parts * tile, features), bf16),
        in_specs=[vmem] * (1 + len(grads)),
        out_specs=vmem,
        scratch_shapes=[pltpu.VMEM((parts, classes, tile), bf16)],
        compiler_params=small_grant,
        name="input_part",
    )(weight, *grads)


def turn_kernel(*refs):
    pieces, (out_ref, held) = refs[:-2], refs[-2:]
    parts, _, tile = held.shape
    join_members(pieces, held)
    for p in range(parts):
        out_ref[p * tile : (p + 1) * tile, :] = held[p].T


def turn(pieces):
    members = len(pieces)
    parts, share, tile = pieces[0].shape
    return pl.pallas_call(
        turn_kernel,
        out_shape=jax.ShapeDtypeStruct((parts * tile, members * share), f32),
        in_specs=[vmem] * members,
        out_specs=vmem,
        scratch_shapes=[pltpu.VMEM((parts, members * share, tile), f32)],
        compiler_params=small_grant,
        name="turn",
    )(*pieces)


def far_first(size):
    half = size // 2
    return [half] + [k for j in range(half - 1, 0, -1) for k in (j, size - j)]


def gather_far(value, axis):
    size = lax.axis_size(axis)
    found = [(lambda mine: mine, value)]
    for k in far_first(size):
        found.append((lambda mine, k=k: lax.rem(mine - k + size, size), shift(value, axis, k)))
    return found


def gather_pairs(value, axis):
    size = lax.axis_size(axis)
    half = size // 2

    def partner(r):
        return r + 1 - 2 * lax.rem(r, 2)

    def turned(r, k):
        return lax.rem(r + 2 * (half - k), size)

    def send(block, k):
        return lax.ppermute(block, axis, [(r, (r + 2 * k) % size) for r in range(size)])

    other = lax.ppermute(value, axis, [(r, r ^ 1) for r in range(size)])
    order = sorted(range(1, half), key=lambda k: -min(k, half - k))
    found = [(lambda mine: mine, value), (partner, other)]
    for block, where in ((value, lambda r: r), (other, partner)):
        for k in order:
            place = lambda mine, k=k, where=where: where(turned(mine, k))
            found.append((place, send(block, k)))
    return found


def add_up(blocks):
    total = blocks[0].astype(f32)
    for block in blocks[1:]:
        total = total + block.astype(f32)
    return total


def per_device(features, weights, tile_values, tile_rows, tile_cols, tile_counts, labels):
    row_count = lax.axis_size("row")
    rep_count = lax.axis_size("rep")
    feats = features[0]
    weight = weights[0]
    slot_values = tile_values[0, 0]
    slot_rows = tile_rows[0, 0]
    slot_cols = tile_cols[0, 0]
    count = tile_counts
    tile = slot_values.shape[1]
    nodes = feats.shape[0]
    parts = nodes // tile
    all_nodes = nodes * row_count * rep_count

    mixed = exchange_relative(project(feats, weight, parts), "member")
    mixed = add_up(mixed).astype(bf16)
    slots = slot_values.shape[0]
    early_slots = slots // unroll * 3 // 4 * unroll
    early = flip(slot_values, 0, early_slots)
    mixed, early, later_values = lax.optimization_barrier((mixed, early, slot_values))
    panel = gather_pairs(mixed, "row")
    sums = tile_pass(
        "forward_tiles",
        panel,
        "row",
        [early, flip(later_values, early_slots, slots - early_slots)],
        slot_rows,
        slot_cols,
        count,
        rep_count * parts,
    )
    sums = lax.all_to_all(sums.reshape(rep_count, parts, -1, tile), "rep", 0, 0)
    logits, grads = grade(labels, sums)
    back = tile_pass(
        "backward_tiles",
        gather_far(grads, "rep"),
        "rep",
        [slot_values],
        slot_cols,
        slot_rows,
        count,
        row_count * parts,
    )
    back = lax.all_to_all(back.reshape(row_count, parts, -1, tile), "row", 0, 0)
    back = jnp.sum(back.astype(f32), axis=0).astype(bf16)
    back = gather_relative(back, "member")
    part = weight_part(feats, back)
    part = lax.all_to_all(part.reshape(-1, 8, 128), ("row", "rep"), 0, 0)
    piece = (jnp.sum(part.astype(f32), axis=0) * (1.0 / math.sqrt(all_nodes))).astype(bf16)
    piece, logits, *back = lax.optimization_barrier((piece, logits, *back))
    spread = lax.all_to_all(jnp.broadcast_to(piece[None], part.shape), ("row", "rep"), 0, 0)
    mean_logits = turn(gather_relative(logits, "member"))
    input_grad = input_part(weight, back)
    features_in, classes = weight.shape
    weight_grad = spread.astype(f32).reshape(features_in // 8, classes // 128, 8, 128)
    weight_grad = weight_grad.transpose(0, 2, 1, 3).reshape(features_in, classes)
    return (mean_logits, weight_grad[None], input_grad[None])


def solution(mesh):
    return jax.shard_map(
        per_device,
        mesh=mesh,
        in_specs=(
            P("member", ("row", "rep"), None),
            P("member", None, None),
            P("row", "rep", None, None, None),
            P("row", "rep", None),
            P("row", "rep", None),
            P("row", "rep"),
            P("row"),
        ),
        out_specs=(
            P(("row", "rep"), None),
            P("member", None, None),
            P("member", ("row", "rep"), None),
        ),
        check_vma=False,
    )
```

```python
import functools
import math

import jax
import jax.numpy as jnp
from jax import lax
from jax.experimental import pallas as pl
from jax.experimental.pallas import tpu as pltpu
from jax.sharding import PartitionSpec as P


bf16 = jnp.bfloat16
f32 = jnp.float32
vmem = pl.BlockSpec(memory_space=pltpu.VMEM)
smem = pl.BlockSpec(memory_space=pltpu.SMEM)
unread = pl.BlockSpec(memory_space=pl.ANY)

unroll = 64
flip_chunks = 8
small_grant = pltpu.CompilerParams(vmem_limit_bytes=6 << 20)
flip_grant = pltpu.CompilerParams(vmem_limit_bytes=44 << 20)
tile_grant = pltpu.CompilerParams(vmem_limit_bytes=8 << 20)


def shift(value, axis, step):
    size = lax.axis_size(axis)
    return lax.ppermute(value, axis, [(j, (j + step) % size) for j in range(size)])


def gather_relative(value, axis):
    size = lax.axis_size(axis)
    return [value] + [shift(value, axis, k) for k in range(1, size)]


def exchange_relative(blocks, axis):
    return [blocks[0]] + [shift(blocks[k], axis, k) for k in range(1, len(blocks))]


def project_kernel(members, parts, feats_ref, weight_ref, *refs):
    outs, held = refs[:members], refs[members]
    mine = lax.axis_index("member")
    tile = feats_ref.shape[0] // parts
    share = weight_ref.shape[1] // members
    for p in range(parts):
        prod = jnp.dot(
            feats_ref[p * tile : (p + 1) * tile, :], weight_ref[...], preferred_element_type=f32
        )
        held[p] = prod.T * (1.0 / members)
    for k in range(members):
        other = lax.rem(mine + k, members)
        first = pl.multiple_of(other * share, share)
        for p in range(parts):
            outs[k][p] = held[p, pl.ds(first, share), :].astype(outs[k].dtype)


def project(feats, weight, parts):
    members = lax.axis_size("member")
    nodes, _ = feats.shape
    classes = weight.shape[1]
    tile = nodes // parts
    share = classes // members
    return pl.pallas_call(
        functools.partial(project_kernel, members, parts),
        out_shape=[jax.ShapeDtypeStruct((parts, share, tile), bf16)] * members,
        in_specs=[vmem, vmem],
        out_specs=[vmem] * members,
        scratch_shapes=[pltpu.VMEM((parts, classes, tile), f32)],
        compiler_params=small_grant,
        name="project",
    )(feats, weight)


def flip_kernel(first, stored, out_ref, held, sems):
    chunks = sems.shape[0]
    size = out_ref.shape[0] // chunks

    def load(chunk):
        return pltpu.make_async_copy(
            stored.at[pl.ds(first + chunk * size, size)],
            held.at[pl.ds(chunk * size, size)],
            sems.at[chunk],
        )

    for chunk in range(chunks):
        load(chunk).start()

    @pl.loop(0, chunks)
    def _(chunk):
        load(chunk).wait()
        for k in range(size):
            slot = chunk * size + k
            out_ref[slot] = held[slot].T


def flip(slot_values, first, slots):
    _, tile, _ = slot_values.shape
    shape = (slots, tile, tile)
    return pl.pallas_call(
        functools.partial(flip_kernel, first),
        out_shape=jax.ShapeDtypeStruct(shape, bf16),
        in_specs=[pl.BlockSpec(memory_space=pl.ANY)],
        out_specs=vmem,
        scratch_shapes=[pltpu.VMEM(shape, bf16), pltpu.SemaphoreType.DMA((flip_chunks,))],
        cost_estimate=pl.CostEstimate(
            flops=0, bytes_accessed=4 * shape[0] * tile * tile, transcendentals=0
        ),
        compiler_params=flip_grant,
        name="flip",
    )(slot_values)


def tile_kernel(offsets, n_tiles, axis_in, put_ref, pick_ref, count_ref, *refs):
    n_in = len(offsets)
    blocks, (out_ref, source, total) = refs[:n_in], refs[-3:]
    tile_refs = refs[n_in : n_in + n_tiles]
    parts = blocks[0].shape[0]
    last = total.shape[0] - 1
    count = count_ref[0, 0]
    mine = lax.axis_index(axis_in)
    for block, offset in zip(blocks, offsets):
        source[pl.ds(offset(mine) * parts, parts)] = block[...]
    total[...] = jnp.zeros_like(total)
    first = 0
    for tiles_ref in tile_refs:
        slots = tiles_ref.shape[0]
        left = jnp.clip(count - first, 0, slots)

        @pl.loop(0, (left + unroll - 1) // unroll)
        def _(group):
            for u in range(unroll):
                local = group * unroll + u
                slot = first + local
                put = jnp.where(slot < count, put_ref[slot], last)
                total[put] += jnp.dot(
                    source[pick_ref[slot]], tiles_ref[local], preferred_element_type=f32
                )

        first += slots

    out_ref[...] = total[:-1].astype(out_ref.dtype)


def tile_pass(name, gathered, axis_in, tiles, put, pick, count, out_tiles, after=()):
    offsets, blocks = zip(*gathered)
    n_in = len(blocks)
    parts, share, tile = blocks[0].shape
    slots = put.shape[0]
    return pl.pallas_call(
        functools.partial(tile_kernel, offsets, len(tiles), axis_in),
        out_shape=jax.ShapeDtypeStruct((out_tiles, share, tile), bf16),
        in_specs=[smem, smem, smem] + [vmem] * (n_in + len(tiles)) + [unread] * len(after),
        out_specs=vmem,
        scratch_shapes=[
            pltpu.VMEM((parts * n_in, share, tile), bf16),
            pltpu.VMEM((out_tiles + 1, share, tile), f32),
        ],
        cost_estimate=pl.CostEstimate(
            flops=2 * slots * tile * tile * share,
            bytes_accessed=slots * tile * tile * 2,
            transcendentals=0,
        ),
        compiler_params=tile_grant,
        name=name,
    )(put, pick, count, *blocks, *tiles, *after)


def grade_kernel(labels_ref, sums_ref, logits_ref, grads_ref):
    parts, share, tile = logits_ref.shape
    first = lax.axis_index("rep") * parts
    classes = lax.broadcasted_iota(jnp.int32, (share, tile), 0) + lax.axis_index("member") * share
    for p in range(parts):
        logits = add_up([sums_ref[k, p] for k in range(sums_ref.shape[0])])
        logits_ref[p] = logits
        target = labels_ref[pl.ds(first + p, 1), :] == classes
        grads_ref[p] = (jax.nn.sigmoid(logits) - target.astype(f32)).astype(grads_ref.dtype)


def grade(labels, sums):
    shape = sums.shape[1:]
    return pl.pallas_call(
        grade_kernel,
        out_shape=[jax.ShapeDtypeStruct(shape, f32), jax.ShapeDtypeStruct(shape, bf16)],
        in_specs=[vmem, vmem],
        out_specs=[vmem, vmem],
        compiler_params=small_grant,
        name="grade",
    )(labels.reshape(-1, shape[2]), sums)


def join_members(pieces, held):
    members = len(pieces)
    mine = lax.axis_index("member")
    parts, share, _ = pieces[0].shape
    for k in range(members):
        owner = lax.rem(mine - k + members, members)
        first = pl.multiple_of(owner * share, share)
        for p in range(parts):
            held[p, pl.ds(first, share), :] = pieces[k][p]


def weight_kernel(feats_ref, *refs):
    grads, (part_ref, held) = refs[:-2], refs[-2:]
    parts, _, tile = held.shape
    join_members(grads, held)
    total = None
    for p in range(parts):
        feats = feats_ref[p * tile : (p + 1) * tile, :]
        term = jnp.dot(held[p], feats, preferred_element_type=f32)
        total = term if total is None else total + term
    total = total.T
    _, halves, _, lanes = part_ref.shape
    for h in range(halves):
        piece = total[:, h * lanes : (h + 1) * lanes].astype(part_ref.dtype)
        part_ref[:, h] = piece.reshape(-1, 8, lanes)


def weight_part(feats, grads):
    parts, share, tile = grads[0].shape
    features, classes = feats.shape[1], share * len(grads)
    return pl.pallas_call(
        weight_kernel,
        out_shape=jax.ShapeDtypeStruct((features // 8, classes // 128, 8, 128), bf16),
        in_specs=[vmem] * (1 + len(grads)),
        out_specs=vmem,
        scratch_shapes=[pltpu.VMEM((parts, classes, tile), bf16)],
        compiler_params=small_grant,
        name="weight_part",
    )(feats, *grads)


def input_kernel(weight_ref, *refs):
    grads, (input_ref, held) = refs[:-2], refs[-2:]
    parts, _, tile = held.shape
    join_members(grads, held)
    for p in range(parts):
        prod = jnp.dot(weight_ref[...], held[p], preferred_element_type=f32)
        input_ref[p * tile : (p + 1) * tile, :] = prod.T.astype(input_ref.dtype)


def input_part(weight, grads):
    parts, share, tile = grads[0].shape
    features, classes = weight.shape
    return pl.pallas_call(
        input_kernel,
        out_shape=jax.ShapeDtypeStruct((parts * tile, features), bf16),
        in_specs=[vmem] * (1 + len(grads)),
        out_specs=vmem,
        scratch_shapes=[pltpu.VMEM((parts, classes, tile), bf16)],
        compiler_params=small_grant,
        name="input_part",
    )(weight, *grads)


def turn_kernel(*refs):
    pieces, (out_ref, held) = refs[:-2], refs[-2:]
    parts, _, tile = held.shape
    join_members(pieces, held)
    for p in range(parts):
        out_ref[p * tile : (p + 1) * tile, :] = held[p].T


def turn(pieces):
    members = len(pieces)
    parts, share, tile = pieces[0].shape
    return pl.pallas_call(
        turn_kernel,
        out_shape=jax.ShapeDtypeStruct((parts * tile, members * share), f32),
        in_specs=[vmem] * members,
        out_specs=vmem,
        scratch_shapes=[pltpu.VMEM((parts, members * share, tile), f32)],
        compiler_params=small_grant,
        name="turn",
    )(*pieces)


def far_first(size):
    half = size // 2
    return [half] + [k for j in range(half - 1, 0, -1) for k in (j, size - j)]


def gather_far(value, axis):
    size = lax.axis_size(axis)
    found = [(lambda mine: mine, value)]
    for k in far_first(size):
        found.append((lambda mine, k=k: lax.rem(mine - k + size, size), shift(value, axis, k)))
    return found


def gather_pairs(value, axis):
    size = lax.axis_size(axis)
    half = size // 2

    def partner(r):
        return r + 1 - 2 * lax.rem(r, 2)

    def turned(r, k):
        return lax.rem(r + 2 * (half - k), size)

    def send(block, k):
        return lax.ppermute(block, axis, [(r, (r + 2 * k) % size) for r in range(size)])

    other = lax.ppermute(value, axis, [(r, r ^ 1) for r in range(size)])
    order = sorted(range(1, half), key=lambda k: -min(k, half - k))
    found = [(lambda mine: mine, value), (partner, other)]
    for block, where in ((value, lambda r: r), (other, partner)):
        for k in order:
            place = lambda mine, k=k, where=where: where(turned(mine, k))
            found.append((place, send(block, k)))
    return found


def add_up(blocks):
    total = blocks[0].astype(f32)
    for block in blocks[1:]:
        total = total + block.astype(f32)
    return total


def per_device(features, weights, tile_values, tile_rows, tile_cols, tile_counts, labels):
    row_count = lax.axis_size("row")
    rep_count = lax.axis_size("rep")
    feats = features[0]
    weight = weights[0]
    slot_values = tile_values[0, 0]
    slot_rows = tile_rows[0, 0]
    slot_cols = tile_cols[0, 0]
    count = tile_counts
    tile = slot_values.shape[1]
    nodes = feats.shape[0]
    parts = nodes // tile
    all_nodes = nodes * row_count * rep_count

    opened = [shift(tile_rows[0], "rep", k) for k in (1, -1)]
    mixed = exchange_relative(project(feats, weight, parts), "member")
    mixed = add_up(mixed).astype(bf16)
    slots = slot_values.shape[0]
    early_slots = slots // unroll * 3 // 4 * unroll
    early = flip(slot_values, 0, early_slots)
    mixed, early, later_values = lax.optimization_barrier((mixed, early, slot_values))
    panel = gather_pairs(mixed, "row")
    sums = tile_pass(
        "forward_tiles",
        panel,
        "row",
        [early, flip(later_values, early_slots, slots - early_slots)],
        slot_rows,
        slot_cols,
        count,
        rep_count * parts,
        opened,
    )
    sums = lax.all_to_all(sums.reshape(rep_count, parts, -1, tile), "rep", 0, 0)
    logits, grads = grade(labels, sums)
    back = tile_pass(
        "backward_tiles",
        gather_far(grads, "rep"),
        "rep",
        [slot_values],
        slot_cols,
        slot_rows,
        count,
        row_count * parts,
    )
    back = lax.all_to_all(back.reshape(row_count, parts, -1, tile), "row", 0, 0)
    back = jnp.sum(back.astype(f32), axis=0).astype(bf16)
    back = gather_relative(back, "member")
    part = weight_part(feats, back)
    part = lax.all_to_all(part.reshape(-1, 8, 128), ("row", "rep"), 0, 0)
    piece = (jnp.sum(part.astype(f32), axis=0) * (1.0 / math.sqrt(all_nodes))).astype(bf16)
    piece, logits, *back = lax.optimization_barrier((piece, logits, *back))
    spread = lax.all_to_all(jnp.broadcast_to(piece[None], part.shape), ("row", "rep"), 0, 0)
    mean_logits = turn(gather_relative(logits, "member"))
    input_grad = input_part(weight, back)
    features_in, classes = weight.shape
    weight_grad = spread.astype(f32).reshape(features_in // 8, classes // 128, 8, 128)
    weight_grad = weight_grad.transpose(0, 2, 1, 3).reshape(features_in, classes)
    return (mean_logits, weight_grad[None], input_grad[None])


def solution(mesh):
    return jax.shard_map(
        per_device,
        mesh=mesh,
        in_specs=(
            P("member", ("row", "rep"), None),
            P("member", None, None),
            P("row", "rep", None, None, None),
            P("row", "rep", None),
            P("row", "rep", None),
            P("row", "rep"),
            P("row"),
        ),
        out_specs=(
            P(("row", "rep"), None),
            P("member", None, None),
            P("member", ("row", "rep"), None),
        ),
        check_vma=False,
    )
```

```python
import functools
import math

import jax
import jax.numpy as jnp
from jax import lax
from jax.experimental import pallas as pl
from jax.experimental.pallas import tpu as pltpu
from jax.sharding import PartitionSpec as P


bf16 = jnp.bfloat16
f32 = jnp.float32
vmem = pl.BlockSpec(memory_space=pltpu.VMEM)
smem = pl.BlockSpec(memory_space=pltpu.SMEM)

unroll = 64
flip_chunks = 8
small_grant = pltpu.CompilerParams(vmem_limit_bytes=6 << 20)
flip_grant = pltpu.CompilerParams(vmem_limit_bytes=44 << 20)
tile_grant = pltpu.CompilerParams(vmem_limit_bytes=8 << 20)


def shift(value, axis, step):
    size = lax.axis_size(axis)
    return lax.ppermute(value, axis, [(j, (j + step) % size) for j in range(size)])


def gather_relative(value, axis):
    size = lax.axis_size(axis)
    return [value] + [shift(value, axis, k) for k in range(1, size)]


def exchange_relative(blocks, axis):
    return [blocks[0]] + [shift(blocks[k], axis, k) for k in range(1, len(blocks))]


def project_kernel(members, parts, feats_ref, weight_ref, *refs):
    outs, held = refs[:members], refs[members]
    mine = lax.axis_index("member")
    tile = feats_ref.shape[0] // parts
    share = weight_ref.shape[1] // members
    for p in range(parts):
        prod = jnp.dot(
            feats_ref[p * tile : (p + 1) * tile, :], weight_ref[...], preferred_element_type=f32
        )
        held[p] = prod.T * (1.0 / members)
    for k in range(members):
        other = lax.rem(mine + k, members)
        first = pl.multiple_of(other * share, share)
        for p in range(parts):
            outs[k][p] = held[p, pl.ds(first, share), :].astype(outs[k].dtype)


def project(feats, weight, parts):
    members = lax.axis_size("member")
    nodes, _ = feats.shape
    classes = weight.shape[1]
    tile = nodes // parts
    share = classes // members
    return pl.pallas_call(
        functools.partial(project_kernel, members, parts),
        out_shape=[jax.ShapeDtypeStruct((parts, share, tile), bf16)] * members,
        in_specs=[vmem, vmem],
        out_specs=[vmem] * members,
        scratch_shapes=[pltpu.VMEM((parts, classes, tile), f32)],
        compiler_params=small_grant,
        name="project",
    )(feats, weight)


def flip_kernel(first, stored, out_ref, held, sems):
    chunks = sems.shape[0]
    size = out_ref.shape[0] // chunks

    def load(chunk):
        return pltpu.make_async_copy(
            stored.at[pl.ds(first + chunk * size, size)],
            held.at[pl.ds(chunk * size, size)],
            sems.at[chunk],
        )

    for chunk in range(chunks):
        load(chunk).start()

    @pl.loop(0, chunks)
    def _(chunk):
        load(chunk).wait()
        for k in range(size):
            slot = chunk * size + k
            out_ref[slot] = held[slot].T


def flip(slot_values, first, slots):
    _, tile, _ = slot_values.shape
    shape = (slots, tile, tile)
    return pl.pallas_call(
        functools.partial(flip_kernel, first),
        out_shape=jax.ShapeDtypeStruct(shape, bf16),
        in_specs=[pl.BlockSpec(memory_space=pl.ANY)],
        out_specs=vmem,
        scratch_shapes=[pltpu.VMEM(shape, bf16), pltpu.SemaphoreType.DMA((flip_chunks,))],
        cost_estimate=pl.CostEstimate(
            flops=0, bytes_accessed=4 * shape[0] * tile * tile, transcendentals=0
        ),
        compiler_params=flip_grant,
        name="flip",
    )(slot_values)


def tile_kernel(offsets, axis_in, put_ref, pick_ref, count_ref, *refs):
    n_in = len(offsets)
    blocks, tile_refs, (out_ref, source, total) = refs[:n_in], refs[n_in:-3], refs[-3:]
    parts = blocks[0].shape[0]
    last = total.shape[0] - 1
    count = count_ref[0, 0]
    mine = lax.axis_index(axis_in)
    for block, offset in zip(blocks, offsets):
        source[pl.ds(offset(mine) * parts, parts)] = block[...]
    total[...] = jnp.zeros_like(total)
    first = 0
    for tiles_ref in tile_refs:
        slots = tiles_ref.shape[0]
        left = jnp.clip(count - first, 0, slots)

        @pl.loop(0, (left + unroll - 1) // unroll)
        def _(group):
            for u in range(unroll):
                local = group * unroll + u
                slot = first + local
                put = jnp.where(slot < count, put_ref[slot], last)
                total[put] += jnp.dot(
                    source[pick_ref[slot]], tiles_ref[local], preferred_element_type=f32
                )

        first += slots

    out_ref[...] = total[:-1].astype(out_ref.dtype)


def tile_pass(name, gathered, axis_in, tiles, put, pick, count, out_tiles):
    offsets, blocks = zip(*gathered)
    n_in = len(blocks)
    parts, share, tile = blocks[0].shape
    slots = put.shape[0]
    return pl.pallas_call(
        functools.partial(tile_kernel, offsets, axis_in),
        out_shape=jax.ShapeDtypeStruct((out_tiles, share, tile), bf16),
        in_specs=[smem, smem, smem] + [vmem] * (n_in + len(tiles)),
        out_specs=vmem,
        scratch_shapes=[
            pltpu.VMEM((parts * n_in, share, tile), bf16),
            pltpu.VMEM((out_tiles + 1, share, tile), f32),
        ],
        cost_estimate=pl.CostEstimate(
            flops=2 * slots * tile * tile * share,
            bytes_accessed=slots * tile * tile * 2,
            transcendentals=0,
        ),
        compiler_params=tile_grant,
        name=name,
    )(put, pick, count, *blocks, *tiles)


def grade_kernel(labels_ref, sums_ref, logits_ref, grads_ref):
    parts, share, tile = logits_ref.shape
    first = lax.axis_index("rep") * parts
    classes = lax.broadcasted_iota(jnp.int32, (share, tile), 0) + lax.axis_index("member") * share
    for p in range(parts):
        logits = add_up([sums_ref[k, p] for k in range(sums_ref.shape[0])])
        logits_ref[p] = logits
        target = labels_ref[pl.ds(first + p, 1), :] == classes
        grads_ref[p] = (jax.nn.sigmoid(logits) - target.astype(f32)).astype(grads_ref.dtype)


def grade(labels, sums):
    shape = sums.shape[1:]
    return pl.pallas_call(
        grade_kernel,
        out_shape=[jax.ShapeDtypeStruct(shape, f32), jax.ShapeDtypeStruct(shape, bf16)],
        in_specs=[vmem, vmem],
        out_specs=[vmem, vmem],
        compiler_params=small_grant,
        name="grade",
    )(labels.reshape(-1, shape[2]), sums)


def join_members(pieces, held):
    members = len(pieces)
    mine = lax.axis_index("member")
    parts, share, _ = pieces[0].shape
    for k in range(members):
        owner = lax.rem(mine - k + members, members)
        first = pl.multiple_of(owner * share, share)
        for p in range(parts):
            held[p, pl.ds(first, share), :] = pieces[k][p]


def weight_kernel(feats_ref, *refs):
    grads, (part_ref, held) = refs[:-2], refs[-2:]
    parts, _, tile = held.shape
    join_members(grads, held)
    total = None
    for p in range(parts):
        feats = feats_ref[p * tile : (p + 1) * tile, :]
        term = jnp.dot(held[p], feats, preferred_element_type=f32)
        total = term if total is None else total + term
    total = total.T
    _, halves, _, lanes = part_ref.shape
    for h in range(halves):
        piece = total[:, h * lanes : (h + 1) * lanes].astype(part_ref.dtype)
        part_ref[:, h] = piece.reshape(-1, 8, lanes)


def weight_part(feats, grads):
    parts, share, tile = grads[0].shape
    features, classes = feats.shape[1], share * len(grads)
    return pl.pallas_call(
        weight_kernel,
        out_shape=jax.ShapeDtypeStruct((features // 8, classes // 128, 8, 128), bf16),
        in_specs=[vmem] * (1 + len(grads)),
        out_specs=vmem,
        scratch_shapes=[pltpu.VMEM((parts, classes, tile), bf16)],
        compiler_params=small_grant,
        name="weight_part",
    )(feats, *grads)


def input_kernel(weight_ref, *refs):
    grads, (input_ref, held) = refs[:-2], refs[-2:]
    parts, _, tile = held.shape
    join_members(grads, held)
    for p in range(parts):
        prod = jnp.dot(weight_ref[...], held[p], preferred_element_type=f32)
        input_ref[p * tile : (p + 1) * tile, :] = prod.T.astype(input_ref.dtype)


def input_part(weight, grads):
    parts, share, tile = grads[0].shape
    features, classes = weight.shape
    return pl.pallas_call(
        input_kernel,
        out_shape=jax.ShapeDtypeStruct((parts * tile, features), bf16),
        in_specs=[vmem] * (1 + len(grads)),
        out_specs=vmem,
        scratch_shapes=[pltpu.VMEM((parts, classes, tile), bf16)],
        compiler_params=small_grant,
        name="input_part",
    )(weight, *grads)


def turn_kernel(*refs):
    pieces, (out_ref, held) = refs[:-2], refs[-2:]
    parts, _, tile = held.shape
    join_members(pieces, held)
    for p in range(parts):
        out_ref[p * tile : (p + 1) * tile, :] = held[p].T


def turn(pieces):
    members = len(pieces)
    parts, share, tile = pieces[0].shape
    return pl.pallas_call(
        turn_kernel,
        out_shape=jax.ShapeDtypeStruct((parts * tile, members * share), f32),
        in_specs=[vmem] * members,
        out_specs=vmem,
        scratch_shapes=[pltpu.VMEM((parts, members * share, tile), f32)],
        compiler_params=small_grant,
        name="turn",
    )(*pieces)


def far_first(size):
    half = size // 2
    return [half] + [k for j in range(half - 1, 0, -1) for k in (j, size - j)]


def gather_far(value, axis):
    size = lax.axis_size(axis)
    found = [(lambda mine: mine, value)]
    for k in far_first(size):
        found.append((lambda mine, k=k: lax.rem(mine - k + size, size), shift(value, axis, k)))
    return found


def gather_pairs(value, axis):
    size = lax.axis_size(axis)
    half = size // 2

    def partner(r):
        return r + 1 - 2 * lax.rem(r, 2)

    def turned(r, k):
        return lax.rem(r + 2 * (half - k), size)

    def send(block, k):
        return lax.ppermute(block, axis, [(r, (r + 2 * k) % size) for r in range(size)])

    other = lax.ppermute(value, axis, [(r, r ^ 1) for r in range(size)])
    order = sorted(range(1, half), key=lambda k: -min(k, half - k))
    found = [(lambda mine: mine, value), (partner, other)]
    for block, where in ((value, lambda r: r), (other, partner)):
        for k in order:
            place = lambda mine, k=k, where=where: where(turned(mine, k))
            found.append((place, send(block, k)))
    return found


def add_up(blocks):
    total = blocks[0].astype(f32)
    for block in blocks[1:]:
        total = total + block.astype(f32)
    return total


def per_device(features, weights, tile_values, tile_rows, tile_cols, tile_counts, labels):
    row_count = lax.axis_size("row")
    rep_count = lax.axis_size("rep")
    feats = features[0]
    weight = weights[0]
    slot_values = tile_values[0, 0]
    slot_rows = tile_rows[0, 0]
    slot_cols = tile_cols[0, 0]
    count = tile_counts
    tile = slot_values.shape[1]
    nodes = feats.shape[0]
    parts = nodes // tile
    all_nodes = nodes * row_count * rep_count

    slots = slot_values.shape[0]
    opening = flip(slot_values, 0, unroll)
    feats_in, weight_in, opening = lax.optimization_barrier((feats, weight, opening))
    mixed = exchange_relative(project(feats_in, weight_in, parts), "member")
    mixed = add_up(mixed).astype(bf16)
    early_slots = slots // unroll * 3 // 4 * unroll
    early = flip(slot_values, unroll, early_slots - unroll)
    mixed, early, later_values = lax.optimization_barrier((mixed, early, slot_values))
    panel = gather_pairs(mixed, "row")
    sums = tile_pass(
        "forward_tiles",
        panel,
        "row",
        [opening, early, flip(later_values, early_slots, slots - early_slots)],
        slot_rows,
        slot_cols,
        count,
        rep_count * parts,
    )
    sums = lax.all_to_all(sums.reshape(rep_count, parts, -1, tile), "rep", 0, 0)
    logits, grads = grade(labels, sums)
    back = tile_pass(
        "backward_tiles",
        gather_far(grads, "rep"),
        "rep",
        [slot_values],
        slot_cols,
        slot_rows,
        count,
        row_count * parts,
    )
    back = lax.all_to_all(back.reshape(row_count, parts, -1, tile), "row", 0, 0)
    back = jnp.sum(back.astype(f32), axis=0).astype(bf16)
    back = gather_relative(back, "member")
    part = weight_part(feats, back)
    part = lax.all_to_all(part.reshape(-1, 8, 128), ("row", "rep"), 0, 0)
    piece = (jnp.sum(part.astype(f32), axis=0) * (1.0 / math.sqrt(all_nodes))).astype(bf16)
    piece, logits, *back = lax.optimization_barrier((piece, logits, *back))
    spread = lax.all_to_all(jnp.broadcast_to(piece[None], part.shape), ("row", "rep"), 0, 0)
    mean_logits = turn(gather_relative(logits, "member"))
    input_grad = input_part(weight, back)
    features_in, classes = weight.shape
    weight_grad = spread.astype(f32).reshape(features_in // 8, classes // 128, 8, 128)
    weight_grad = weight_grad.transpose(0, 2, 1, 3).reshape(features_in, classes)
    return (mean_logits, weight_grad[None], input_grad[None])


def solution(mesh):
    return jax.shard_map(
        per_device,
        mesh=mesh,
        in_specs=(
            P("member", ("row", "rep"), None),
            P("member", None, None),
            P("row", "rep", None, None, None),
            P("row", "rep", None),
            P("row", "rep", None),
            P("row", "rep"),
            P("row"),
        ),
        out_specs=(
            P(("row", "rep"), None),
            P("member", None, None),
            P("member", ("row", "rep"), None),
        ),
        check_vma=False,
    )
```
